128 devices in a mesh: node: 4 (over x), intra: 32 (over z, y, core).
Axes of the slice: x: 4, y: 4, z: 4, core: 2. Of those that a mesh axis runs over, the one named last changes fastest.
Arguments:
- gradients: bfloat16 [4, 32, 12288, 512], P('node', 'intra'), as said below
- sign_table: int32 [64, 512], replicated, may hold values from -1 to 1, as said below
- loss_scale: float32 [1], replicated, may hold values from 256 to 65536
- step_count: int32 [1], replicated, may hold values from 1 to 8
- weights: float32 [12288, 512], P('intra', 'node'), may hold values from -6 to 6
- first_moment: float32 [12288, 512], P('intra', 'node'), may hold values from -3 to 3
- second_moment: float32 [12288, 512], P('intra', 'node'), may hold values from 0.01 to 0.1
Outputs:
- new_weights: float32 [12288, 512], P('intra', 'node')
- new_first: float32 [12288, 512], P('intra', 'node')
- new_second: float32 [12288, 512], P('intra', 'node')
The draws below stay inside these ranges and needn't reach their ends.
Inputs may be any that keep to these rules, and one draw needn't show every extreme that they name: `gradients`: each replica's gradient is multiplied by loss_scale. `sign_table`: every entry is -1 or 1.
All inputs are finite; a program needn't handle non-finite values.
Results may differ from the reference program's by a relative error of at most 0.0003.
Values sent between devices are 32-bit elements; how exact they have to be, the bound alone decides.
No kernel may reach another device: no remote copies, remote signals or barrier semaphores. Data moves between devices by JAX's collectives and lax.ppermute only.
A program may use at most 128 MiB of HBM per device.

```python
import math
import jax
import jax.numpy as jnp
from jax import lax

BLOCK = 128
SIGN_ROWS = 64
GRAD_ROWS = 12288
GRAD_COLS = 512
N_NODE = 4
N_INTRA = 32


def shared_scale(key):
    fraction = jax.random.uniform(jax.random.fold_in(key, 11), (), jnp.float32)
    return jnp.exp(jnp.log(256.0) + fraction * (jnp.log(65536.0) - jnp.log(256.0)))


def draw_loss_scale(key, part):
    return shared_scale(key).reshape(1).astype(jnp.float32)


def draw_gradients(key, part):
    replicas = N_NODE * N_INTRA
    ranking = jnp.arange(replicas, dtype=jnp.float32) / (replicas - 1)
    jitter = jax.random.uniform(jax.random.fold_in(key, 1), (replicas,), jnp.float32, 0.8, 1.25)
    device_scale = jnp.power(3.0, ranking) * jitter
    noise = jax.random.truncated_normal(jax.random.fold_in(key, 2), -6.0, 6.0, (replicas, GRAD_ROWS, GRAD_COLS), jnp.float32)
    values = noise * device_scale[:, None, None] * shared_scale(key)
    return values.reshape(N_NODE, N_INTRA, GRAD_ROWS, GRAD_COLS).astype(jnp.bfloat16)


def draw_sign_table(key, part):
    return 2 * jax.random.randint(jax.random.fold_in(key, 21), (SIGN_ROWS, GRAD_COLS), 0, 2, jnp.int32) - 1


def level_of(rng, dims, cuts, low, high):
    def one(position, blocks):
        steps = jax.random.uniform(jax.random.fold_in(jax.random.fold_in(rng, 6), position), (blocks,), jnp.float32, low / len(cuts), high / len(cuts))
        return jnp.repeat(jnp.exp(steps), dims[position] // blocks).reshape((-1,) + (1,) * (len(dims) - position - 1))

    loudness = one(*cuts[0])
    for cut in cuts[1:]:
        loudness = loudness * one(*cut)
    return loudness


def bell_draw(key, shape, scale, most, cuts=(), held_as=jnp.bfloat16):
    level = level_of(key, shape, cuts, -0.22, 0.18) if cuts else 1.0
    array = jax.random.normal(key, shape, jnp.float32) * scale * level
    return jnp.minimum(jnp.maximum(array, -most), most).astype(held_as)


def setup_inputs(seed: int = 0) -> dict:
    arg_keys = jax.random.split(jax.random.key(seed), 8)
    return {
        "gradients": draw_gradients(jax.random.fold_in(arg_keys[7], 71), 0),
        "sign_table": draw_sign_table(jax.random.fold_in(arg_keys[7], 71), 0),
        "loss_scale": draw_loss_scale(jax.random.fold_in(arg_keys[7], 71), 0),
        "step_count": jax.random.randint(arg_keys[3], (1,), 1, 9).astype(jnp.int32),
        "weights": bell_draw(arg_keys[4], (GRAD_ROWS, GRAD_COLS), 1.0, 6.0, ((0, 32), (1, 4)), jnp.float32),
        "first_moment": bell_draw(arg_keys[5], (GRAD_ROWS, GRAD_COLS), 0.2, 3.0, ((0, 32), (1, 4)), jnp.float32),
        "second_moment": jnp.clip(jnp.exp(math.log(0.1) - 2.3025851 * jax.random.uniform(arg_keys[6], (GRAD_ROWS, GRAD_COLS), jnp.float32) ** level_of(arg_keys[6], (GRAD_ROWS, GRAD_COLS), ((0, 32), (1, 4)), -0.2, 0.2)), 0.01, 0.1),
    }


def hadamard(order):
    index = jnp.arange(order, dtype=jnp.int32)
    common = index[:, None] & index[None, :]
    parity = jnp.zeros((order, order), jnp.int32)
    for bit_index in range(order.bit_length() - 1):
        parity = parity ^ common >> bit_index & 1
    return 1 - 2 * parity

def reference(gradients, sign_table, loss_scale, step_count, weights, first_moment, second_moment):
    table_int = hadamard(BLOCK)
    table_half = table_int.astype(jnp.bfloat16)
    table_full = table_int.astype(jnp.float32)
    inverse_root = 1.0 / math.sqrt(BLOCK)
    sign_tile = jnp.tile(sign_table, (GRAD_ROWS // SIGN_ROWS, 1))
    sign_half = sign_tile.astype(jnp.bfloat16)
    replicas = gradients.reshape(N_NODE * N_INTRA, GRAD_ROWS, GRAD_COLS)

    def rotate(replica):
        signed = (replica * sign_half).reshape(-1, BLOCK)
        spun = jnp.dot(signed, table_half, preferred_element_type=jnp.float32) * inverse_root
        return spun.reshape(GRAD_ROWS, GRAD_COLS)
    maxima = lax.map(lambda replica: jnp.max(jnp.abs(rotate(replica))), replicas)
    top_value = jnp.max(maxima)
    level_scale = 127.0 / top_value

    def accumulate(carry, replica):
        levels = jnp.floor(rotate(replica) * level_scale + 0.5)
        return (carry + levels, None)
    summed, _ = lax.scan(accumulate, jnp.zeros((GRAD_ROWS, GRAD_COLS), jnp.float32), replicas)
    factor = top_value / (127.0 * (N_NODE * N_INTRA) * loss_scale[0])
    scaled = (summed * factor).reshape(-1, BLOCK)
    back = jnp.dot(scaled, table_full, precision=lax.Precision.HIGHEST) * inverse_root
    grad = back.reshape(GRAD_ROWS, GRAD_COLS) * sign_tile.astype(jnp.float32)
    new_first = 0.9 * first_moment + 0.1 * grad
    new_second = 0.95 * second_moment + 0.05 * grad * grad
    steps_float = step_count[0].astype(jnp.float32)
    first_hat = new_first / (1.0 - jnp.power(jnp.float32(0.9), steps_float))
    second_hat = new_second / (1.0 - jnp.power(jnp.float32(0.95), steps_float))
    update = first_hat / (jnp.sqrt(second_hat) + 1e-08) + 0.1 * weights
    new_weights = weights - 0.2 * update
    return (new_weights, new_first, new_second)
```

```python
import functools
import math

import jax
import jax.numpy as jnp
from jax import lax
from jax.experimental import pallas as pl
from jax.experimental.pallas import tpu as pltpu
from jax.sharding import Mesh
from jax.sharding import PartitionSpec as P

BLOCK = 128
SIGN_ROWS = 64
ROOT = 1.0 / math.sqrt(BLOCK)
CHIPS = ("x", "z", "y")
ALL = ("x", "z", "y", "core")
INTRA = ("z", "y", "core")
FIRST = ("x", "y", "z")
FIELD = 4096.0
F32 = jnp.float32
BF16 = jnp.bfloat16


def hadamard(order):
    index = jnp.arange(order, dtype=jnp.int32)
    common = index[:, None] & index[None, :]
    parity = jnp.zeros((order, order), jnp.int32)
    for bit_index in range(order.bit_length() - 1):
        parity = parity ^ common >> bit_index & 1
    return 1 - 2 * parity


def rotate(block, signs, table):
    signed = block * signs
    halves = [
        jnp.dot(signed[:, 256 * h : 256 * h + 256], table, preferred_element_type=F32)
        for h in range(2)
    ]
    return jnp.concatenate(halves, axis=1) * ROOT


def rotate_kernel(place, own_ref, other_ref, sign_ref, table_ref, raw_ref, top_ref):
    signs = jnp.concatenate([sign_ref[...]] * 2, axis=0)
    table = table_ref[...]

    @pl.when(pl.program_id(0) == 0)
    def _():
        top_ref[...] = jnp.zeros_like(top_ref)

    def fold(value):
        return jnp.max(jnp.abs(value).reshape(-1, 8, 512), axis=0)

    best = jnp.zeros((8, 512), F32)
    for y in range(4):
        best = jnp.maximum(best, fold(rotate(own_ref[0, y, 0, 0], signs, table)))
        other = rotate(other_ref[0, y, 0, 0], signs, table)
        raw_ref[0, y] = other
        best = jnp.maximum(best, fold(other))
    top_ref[...] = jnp.maximum(top_ref[...], best)


def rotate_third(third, place, grads, signs, table):
    view = grads.reshape(4, 4, 2, 3, 128, 512)
    block = (1, 4, 1, 1, 128, 512)
    return pl.pallas_call(
        rotate_kernel,
        grid_spec=pltpu.PrefetchScalarGridSpec(
            num_scalar_prefetch=1,
            grid=(4,),
            in_specs=[
                pl.BlockSpec(block, lambda i, p: (i, 0, p[0], third, 0, 0)),
                pl.BlockSpec(block, lambda i, p: (i, 0, 1 - p[0], third, 0, 0)),
                pl.BlockSpec((64, 512), lambda i, p: (0, 0)),
                pl.BlockSpec((256, 256), lambda i, p: (0, 0)),
            ],
            out_specs=[
                pl.BlockSpec((1, 4, 128, 512), lambda i, p: (i, 0, 0, 0)),
                pl.BlockSpec((8, 512), lambda i, p: (0, 0)),
            ],
        ),
        out_shape=[
            jax.ShapeDtypeStruct((4, 4, 128, 512), F32),
            jax.ShapeDtypeStruct((8, 512), F32),
        ],
        compiler_params=pltpu.CompilerParams(vmem_limit_bytes=40 * 2**20),
        cost_estimate=pl.CostEstimate(flops=2 * 10**9, bytes_accessed=9 * 10**6, transcendentals=0),
    )(place, view, view, signs, table)


def spread_kernel(a_ref, b_ref, c_ref, out_ref):
    best = jnp.maximum(jnp.maximum(a_ref[...], b_ref[...]), c_ref[...])
    out_ref[...] = jnp.broadcast_to(jnp.max(best, axis=(0, 1), keepdims=True), (128, 128))


def level_kernel(
    place, own0, own1, own2, raw0, raw1, raw2, sign0, sign1, sign2, table_ref, top_ref, out0, out1, out2
):
    table = table_ref[...]
    scale = 127.0 / jnp.max(top_ref[...], axis=(0, 1), keepdims=True)
    for own, raw, sign, out in ((own0, raw0, sign0, out0), (own1, raw1, sign1, out1), (own2, raw2, sign2, out2)):
        signs = sign[...]
        for y in range(4):
            mine = rotate(own[0, y, 0, 0], signs, table)
            total = jnp.floor(mine * scale + 0.5) + jnp.floor(raw[0, y] * scale + 0.5)
            word = total[:16] + FIELD * total[16:]
            for x in range(4):
                out[x, 0, y] = word[:, 128 * x : 128 * x + 128]


def levels_for(place, grads, raws, signs, table, tops):
    view = grads.reshape(4, 4, 2, 12, 32, 512)
    own = [
        pl.BlockSpec((1, 4, 1, 1, 32, 512), lambda i, p, t=t: (i, 0, p[0], 4 * t + p[1 + t], 0, 0))
        for t in range(3)
    ]
    raw = [pl.BlockSpec((1, 4, 32, 512), lambda i, p, t=t: (i, 0, p[1 + t], 0)) for t in range(3)]
    sign = [pl.BlockSpec((32, 512), lambda i, p, t=t: (lax.rem(p[1 + t], 2), 0)) for t in range(3)]
    return pl.pallas_call(
        level_kernel,
        grid_spec=pltpu.PrefetchScalarGridSpec(
            num_scalar_prefetch=1,
            grid=(4,),
            in_specs=own
            + raw
            + sign
            + [
                pl.BlockSpec((256, 256), lambda i, p: (0, 0)),
                pl.BlockSpec((128, 128), lambda i, p: (0, 0)),
            ],
            out_specs=[pl.BlockSpec((4, 1, 4, 16, 128), lambda i, p: (0, i, 0, 0, 0))] * 3,
        ),
        out_shape=[jax.ShapeDtypeStruct((4, 4, 4, 16, 128), F32)] * 3,
        compiler_params=pltpu.CompilerParams(vmem_limit_bytes=40 * 2**20),
        cost_estimate=pl.CostEstimate(flops=10**9, bytes_accessed=6 * 10**6, transcendentals=0),
    )(place, view, view, view, *raws, signs, signs, signs, table, tops)


def gather_kernel(*refs):
    out = refs[-1]
    for t in range(3):
        a, b, c, d = (refs[4 * t + k][0] for k in range(4))
        out[:, 16 * t : 16 * t + 16, :] = ((a + b) + (c + d)).reshape(16, 16, 128)


def sum_four(parts):
    return pl.pallas_call(
        gather_kernel,
        grid=(4,),
        in_specs=[pl.BlockSpec((1, 4, 4, 16, 128), lambda i: (i, 0, 0, 0, 0))] * 12,
        out_specs=pl.BlockSpec((16, 48, 128), lambda i: (i, 0, 0)),
        out_shape=jax.ShapeDtypeStruct((64, 48, 128), F32),
        compiler_params=pltpu.CompilerParams(vmem_limit_bytes=40 * 2**20),
        cost_estimate=pl.CostEstimate(flops=10**6, bytes_accessed=8 * 10**6, transcendentals=0),
    )(*parts)


def update_kernel(
    scalars, words_ref, table_ref, sign_ref, weights_ref, first_ref, second_ref, weights_out, first_out, second_out
):
    table = table_ref[...]
    for t in range(3):
        for q in range(4):
            parts = []
            for a in range(4):
                for b in range(4):
                    x, z, y = ((q, a, b), (a, b, q), (a, q, b))[t]
                    parts.append(words_ref[x, z, y, 16 * t : 16 * t + 16, :])
            low = high = jnp.zeros((16, 128), F32)
            for word in parts:
                upper = jnp.floor(word * (1.0 / FIELD) + 0.5)
                high = high + upper
                low = low + (word - upper * FIELD)
            total = jnp.concatenate([low, high], axis=0)
            coarse = jnp.floor(total * (1.0 / 128.0) + 0.5)
            fine = total - coarse * 128.0
            back = 128.0 * jnp.dot(coarse.astype(BF16), table, preferred_element_type=F32) + jnp.dot(
                fine.astype(BF16), table, preferred_element_type=F32
            )
            rows = pl.ds(128 * t + 32 * q, 32)
            grad = (back * scalars[0]) * ROOT * sign_ref[pl.ds(32 * (q % 2), 32), :].astype(F32)
            first = 0.9 * first_ref[rows, :] + 0.1 * grad
            second = 0.95 * second_ref[rows, :] + 0.05 * grad * grad
            weights = weights_ref[rows, :]
            update = (first / scalars[1]) / (jnp.sqrt(second / scalars[2]) + 1e-08) + 0.1 * weights
            weights_out[rows, :] = weights - 0.2 * update
            first_out[rows, :] = first
            second_out[rows, :] = second


def shift(amount):
    return [(i, (i + amount) % 4) for i in range(4)]


def shards(gradients, sign_table, loss_scale, step_count, weights, first_moment, second_moment):
    grads = gradients[0, 0]
    table = hadamard(BLOCK).astype(BF16)
    empty = jnp.zeros_like(table)
    twice = jnp.block([[table, empty], [empty, table]])
    signs = sign_table.astype(BF16)
    core = lax.axis_index("core")
    here = [lax.axis_index(axis) for axis in FIRST]

    place = core.reshape(1)
    raws, tops = [], []
    for third in range(3):
        raw, top = rotate_third(third, place, grads, signs, twice)
        raws.append(lax.ppermute(raw, "core", [(0, 1), (1, 0)]))
        tops.append(top)
    top_tile = pl.pallas_call(spread_kernel, out_shape=jax.ShapeDtypeStruct((128, 128), F32))(*tops)
    tops = lax.all_to_all(top_tile, ALL, 0, 0, tiled=True)

    parts = [[] for _ in range(3)]
    for offset in (2, 1, 3, 0):
        quarter = [lax.rem(h + offset, 4) for h in here]
        outs = levels_for(jnp.stack([core, *quarter]), grads, raws, signs, twice, tops)
        for third, out in enumerate(outs):
            parts[third].append(lax.ppermute(out, FIRST[third], shift(offset)) if offset else out)
    words = sum_four([part for third in parts for part in third])
    words = lax.all_to_all(words, CHIPS, 0, 0, tiled=True)

    top_value = jnp.max(tops)
    factor = top_value / (127.0 * 128.0 * loss_scale[0])
    steps_float = step_count[0].astype(F32)
    scalars = jnp.stack(
        [
            factor,
            1.0 - jnp.power(F32(0.9), steps_float),
            1.0 - jnp.power(F32(0.95), steps_float),
        ]
    )
    own_signs = lax.dynamic_slice_in_dim(sign_table, lax.axis_index("x") * BLOCK, BLOCK, 1)
    vmem = pl.BlockSpec(memory_space=pltpu.VMEM)
    return pl.pallas_call(
        update_kernel,
        in_specs=[pl.BlockSpec(memory_space=pltpu.SMEM)] + [vmem] * 6,
        out_specs=[vmem] * 3,
        out_shape=[jax.ShapeDtypeStruct((384, 128), F32)] * 3,
        compiler_params=pltpu.CompilerParams(vmem_limit_bytes=40 * 2**20),
    )(scalars, words.reshape(4, 4, 4, 48, 128), table, own_signs, weights, first_moment, second_moment)


def solution(mesh):
    torus = Mesh(mesh.devices.reshape(4, 4, 4, 2), ("x", "z", "y", "core"))
    owned = P(INTRA, "x")
    return jax.shard_map(
        shards,
        mesh=torus,
        in_specs=(P("x", INTRA, None, None), P(), P(), P(), owned, owned, owned),
        out_specs=(owned, owned, owned),
        check_vma=False,
    )
```

```python
import functools
import math

import jax
import jax.numpy as jnp
import numpy as np
from jax import lax
from jax.experimental import pallas as pl
from jax.experimental.pallas import tpu as pltpu
from jax.sharding import Mesh
from jax.sharding import PartitionSpec as P

BLOCK = 128
SIGN_ROWS = 64
ROOT = 1.0 / math.sqrt(BLOCK)
CHIPS = ("x", "z", "y")
ALL = ("x", "z", "y", "core")
INTRA = ("z", "y", "core")
FIRST = ("x", "y", "z")
FIELD = 4096.0
F32 = jnp.float32
BF16 = jnp.bfloat16


def hadamard(order):
    table = np.ones((1, 1), np.float32)
    while table.shape[0] < order:
        table = np.block([[table, table], [table, -table]])
    return table


def rotate_kernel(grads_ref, sign_ref, table_ref, raw0, raw1, raw2, own_ref, top_ref, buffer, sems):
    core = lax.axis_index("core")
    copies = [pltpu.make_async_copy(grads_ref.at[i], buffer.at[i], sems.at[i]) for i in range(16)]
    for copy in copies:
        copy.start()
    signs = sign_ref[...].astype(F32).astype(BF16)
    table = table_ref[...]

    def fold(value):
        return jnp.max(jnp.abs(value).reshape(-1, 8, 256), axis=0)

    best = jnp.zeros((8, 256), F32)
    for i in range(16):
        copies[i].wait()

        for third, raw_ref in enumerate((raw0, raw1, raw2)):
            rows = pl.ds(128 * third, 128)
            wide = jnp.concatenate([signs, signs], axis=0)
            mine = buffer[i, core, rows, :] * wide
            own_ref[i, rows, :] = mine
            other = buffer[i, 1 - core, rows, :] * wide
            block = jnp.concatenate([v[:, 256 * h : 256 * h + 256] for v in (other, mine) for h in range(2)], axis=0)
            turned = jnp.dot(block, table, preferred_element_type=F32) * ROOT
            raw_ref[i, :, :256] = turned[:128]
            raw_ref[i, :, 256:] = turned[128:256]
            best = jnp.maximum(best, fold(turned))
    top_ref[...] = jnp.broadcast_to(jnp.max(best, axis=(0, 1), keepdims=True), (128, 128))


VMEM = pl.BlockSpec(memory_space=pltpu.VMEM)


def rotate_all(grads, signs, table):
    return pl.pallas_call(
        rotate_kernel,
        in_specs=[pl.BlockSpec(memory_space=pl.ANY), VMEM, VMEM],
        out_specs=[VMEM] * 5,
        out_shape=[pltpu.VMEM((16, 128, 512), F32)] * 3
        + [
            pltpu.VMEM((16, 384, 512), BF16),
            jax.ShapeDtypeStruct((128, 128), F32),
        ],
        scratch_shapes=[pltpu.VMEM((16, 2, 384, 512), BF16), pltpu.SemaphoreType.DMA((16,))],
        compiler_params=pltpu.CompilerParams(vmem_limit_bytes=40 * 2**20),
        cost_estimate=pl.CostEstimate(flops=6 * 10**9, bytes_accessed=12 * 10**6, transcendentals=0),
    )(grads.reshape(16, 2, 384, 512), signs, table)


def level_kernel(offset, own_ref, raw0, raw1, raw2, table_ref, top_ref, *outs):
    table = table_ref[...]
    scale = 127.0 / jnp.max(top_ref[...], axis=(0, 1), keepdims=True)
    ahead = jnp.where(lax.axis_index("core") == 0, offset, 4 - offset)
    quarters = [lax.rem(lax.axis_index(axis) + ahead, 4) for axis in FIRST]
    raws = (raw0, raw1, raw2)

    def plane(z, carry):
        blocks = [own_ref[4 * z + y, 4 * t + quarters[t]] for t in range(3) for y in range(4)]
        stacked = jnp.concatenate([v[:, 256 * h : 256 * h + 256] for v in blocks for h in range(2)], axis=0)
        mine = jnp.dot(stacked, table, preferred_element_type=F32) * ROOT
        mine = jnp.floor(mine * scale + 0.5)
        for t in range(3):
            for y in range(4):
                for h in range(2):
                    row = 32 * ((t * 4 + y) * 2 + h)
                    other = raws[t][4 * z + y, quarters[t], :, 256 * h : 256 * h + 256]
                    total = mine[row : row + 32] + jnp.floor(other * scale + 0.5)
                    word = total[:16] + FIELD * total[16:]
                    for x in range(2):
                        outs[t][2 * h + x, z, y] = word[:, 128 * x : 128 * x + 128]
        return carry

    lax.fori_loop(0, 4, plane, 0)


def levels_for(offset, own, raws, table, tops):
    return pl.pallas_call(
        functools.partial(level_kernel, offset),
        in_specs=[VMEM] * 6,
        out_specs=[VMEM] * 3,
        out_shape=[pltpu.VMEM((4, 4, 4, 16, 128), F32)] * 3,
        compiler_params=pltpu.CompilerParams(vmem_limit_bytes=12 * 2**20),
        cost_estimate=pl.CostEstimate(flops=10**9, bytes_accessed=6 * 10**6, transcendentals=0),
    )(own.reshape(16, 12, 32, 512), *[raw.reshape(16, 4, 32, 512) for raw in raws], table, tops)


def gather_kernel(*refs):
    out = refs[-1]

    def some(i, carry):
        for t in range(3):
            a, b, c, d = (refs[4 * t + k][pl.ds(8 * i, 8)] for k in range(4))
            out[pl.ds(8 * i, 8), 16 * t : 16 * t + 16, :] = (a + b) + (c + d)
        return carry

    lax.fori_loop(0, 8, some, 0)


def sum_four(parts):
    return pl.pallas_call(
        gather_kernel,
        in_specs=[VMEM] * 12,
        out_specs=VMEM,
        out_shape=pltpu.VMEM((64, 48, 128), F32),
        compiler_params=pltpu.CompilerParams(vmem_limit_bytes=12 * 2**20),
        cost_estimate=pl.CostEstimate(flops=10**6, bytes_accessed=8 * 10**6, transcendentals=0),
    )(*[part.reshape(64, 16, 128) for part in parts])


def update_kernel(
    scalars, words_ref, table_ref, sign_ref, weights_ref, first_ref, second_ref, weights_out, first_out, second_out
):
    table = table_ref[...]
    for t in range(3):
        for q in range(4):
            parts = []
            for a in range(4):
                for b in range(4):
                    x, z, y = ((q, a, b), (a, b, q), (a, q, b))[t]
                    parts.append(words_ref[x, z, y, 16 * t : 16 * t + 16, :])
            low = high = jnp.zeros((16, 128), F32)
            for word in parts:
                upper = jnp.floor(word * (1.0 / FIELD) + 0.5)
                high = high + upper
                low = low + (word - upper * FIELD)
            total = jnp.concatenate([low, high], axis=0)
            coarse = jnp.floor(total * (1.0 / 128.0) + 0.5)
            fine = total - coarse * 128.0
            back = 128.0 * jnp.dot(coarse.astype(BF16), table, preferred_element_type=F32) + jnp.dot(
                fine.astype(BF16), table, preferred_element_type=F32
            )
            rows = pl.ds(128 * t + 32 * q, 32)
            grad = (back * scalars[0]) * ROOT * sign_ref[pl.ds(32 * (q % 2), 32), :].astype(F32)
            first = 0.9 * first_ref[rows, :] + 0.1 * grad
            second = 0.95 * second_ref[rows, :] + 0.05 * grad * grad
            weights = weights_ref[rows, :]
            update = (first / scalars[1]) / (jnp.sqrt(second / scalars[2]) + 1e-08) + 0.1 * weights
            weights_out[rows, :] = weights - 0.2 * update
            first_out[rows, :] = first
            second_out[rows, :] = second


def shift(amount):
    return [
        (2 * i + core, 2 * ((i + (amount if core == 0 else -amount)) % 4) + core)
        for i in range(4)
        for core in range(2)
    ]


def shards(gradients, sign_table, loss_scale, step_count, weights, first_moment, second_moment):
    grads = gradients[0, 0]
    table = jnp.asarray(hadamard(BLOCK), BF16)
    twice = jnp.asarray(np.kron(np.eye(2, dtype=np.float32), hadamard(BLOCK)), BF16)
    *raws, own, top_tile = rotate_all(grads, sign_table, twice)
    raws = [lax.ppermute(raw, "core", [(0, 1), (1, 0)]) for raw in raws]
    tops = lax.all_to_all(top_tile, ALL, 0, 0, tiled=True)

    parts = [[] for _ in range(3)]
    for offset in (1, 3, 2, 0):
        outs = levels_for(offset, own, raws, twice, tops)
        for third, out in enumerate(outs):
            parts[third].append(lax.ppermute(out, (FIRST[third], "core"), shift(offset)) if offset else out)
    words = sum_four([part for third in parts for part in third])
    words = lax.all_to_all(words, CHIPS, 0, 0, tiled=True)

    top_value = jnp.max(tops)
    factor = top_value / (127.0 * 128.0 * loss_scale[0])
    steps_float = step_count[0].astype(F32)
    scalars = jnp.stack(
        [
            factor,
            1.0 - jnp.power(F32(0.9), steps_float),
            1.0 - jnp.power(F32(0.95), steps_float),
        ]
    )
    own_signs = lax.dynamic_slice_in_dim(sign_table, lax.axis_index("x") * BLOCK, BLOCK, 1)
    return pl.pallas_call(
        update_kernel,
        in_specs=[pl.BlockSpec(memory_space=pltpu.SMEM)] + [VMEM] * 6,
        out_specs=[VMEM] * 3,
        out_shape=[jax.ShapeDtypeStruct((384, 128), F32)] * 3,
        compiler_params=pltpu.CompilerParams(vmem_limit_bytes=40 * 2**20),
    )(scalars, words.reshape(4, 4, 4, 48, 128), table, own_signs, weights, first_moment, second_moment)


def solution(mesh):
    torus = Mesh(mesh.devices.reshape(4, 4, 4, 2), ("x", "z", "y", "core"))
    owned = P(INTRA, "x")
    return jax.shard_map(
        shards,
        mesh=torus,
        in_specs=(P("x", INTRA, None, None), P(), P(), P(), owned, owned, owned),
        out_specs=(owned, owned, owned),
        check_vma=False,
    )
```

```python
import functools
import math

import jax
import jax.numpy as jnp
import numpy as np
from jax import lax
from jax.experimental import pallas as pl
from jax.experimental.pallas import tpu as pltpu
from jax.sharding import Mesh
from jax.sharding import PartitionSpec as P

BLOCK = 128
SIGN_ROWS = 64
ROOT = 1.0 / math.sqrt(BLOCK)
CHIPS = ("z", "y", "x")
ALL = ("z", "y", "x", "core")
INTRA = ("z", "y", "core")
FIRST = ("x", "y", "z")
FIELD = 4096.0
F32 = jnp.float32
BF16 = jnp.bfloat16


def hadamard(order):
    table = np.ones((1, 1), np.float32)
    while table.shape[0] < order:
        table = np.block([[table, table], [table, -table]])
    return table


def rotate_kernel(grads_ref, sign_ref, table_ref, raw0, raw1, raw2, own_ref, top_ref, buffer, sems):
    core = lax.axis_index("core")
    copies = [pltpu.make_async_copy(grads_ref.at[i], buffer.at[i], sems.at[i]) for i in range(16)]
    for copy in copies:
        copy.start()
    signs = sign_ref[...].astype(F32).astype(BF16)
    table = table_ref[...]

    def fold(value):
        return jnp.max(jnp.abs(value).reshape(-1, 8, 256), axis=0)

    best = jnp.zeros((8, 256), F32)
    for i in range(16):
        copies[i].wait()

        for third, raw_ref in enumerate((raw0, raw1, raw2)):
            rows = pl.ds(128 * third, 128)
            wide = jnp.concatenate([signs, signs], axis=0)
            mine = buffer[i, core, rows, :] * wide
            own_ref[i, rows, :] = mine
            other = buffer[i, 1 - core, rows, :] * wide
            block = jnp.concatenate([v[:, 256 * h : 256 * h + 256] for v in (other, mine) for h in range(2)], axis=0)
            turned = jnp.dot(block, table, preferred_element_type=F32) * ROOT
            raw_ref[i, :, :256] = turned[:128]
            raw_ref[i, :, 256:] = turned[128:256]
            best = jnp.maximum(best, fold(turned))
    top_ref[...] = jnp.broadcast_to(jnp.max(best, axis=(0, 1), keepdims=True), (128, 128))


VMEM = pl.BlockSpec(memory_space=pltpu.VMEM)


def rotate_all(grads, signs, table):
    return pl.pallas_call(
        rotate_kernel,
        in_specs=[pl.BlockSpec(memory_space=pl.ANY), VMEM, VMEM],
        out_specs=[VMEM] * 5,
        out_shape=[pltpu.VMEM((16, 128, 512), F32)] * 3
        + [
            pltpu.VMEM((16, 384, 512), BF16),
            jax.ShapeDtypeStruct((128, 128), F32),
        ],
        scratch_shapes=[pltpu.VMEM((16, 2, 384, 512), BF16), pltpu.SemaphoreType.DMA((16,))],
        compiler_params=pltpu.CompilerParams(vmem_limit_bytes=40 * 2**20),
        cost_estimate=pl.CostEstimate(flops=6 * 10**9, bytes_accessed=12 * 10**6, transcendentals=0),
    )(grads.reshape(16, 2, 384, 512), signs, table)


def level_kernel(offset, own_ref, raw0, raw1, raw2, table_ref, top_ref, *outs):
    table = table_ref[...]
    scale = 127.0 / jnp.max(top_ref[...], axis=(0, 1), keepdims=True)
    ahead = jnp.where(lax.axis_index("core") == 0, offset, 4 - offset)
    quarters = [lax.rem(lax.axis_index(axis) + ahead, 4) for axis in FIRST]
    raws = (raw0, raw1, raw2)

    def plane(z, carry):
        blocks = [own_ref[4 * z + y, 4 * t + quarters[t]] for t in range(3) for y in range(4)]
        stacked = jnp.concatenate([v[:, 256 * h : 256 * h + 256] for v in blocks for h in range(2)], axis=0)
        mine = jnp.dot(stacked, table, preferred_element_type=F32) * ROOT
        mine = jnp.floor(mine * scale + 0.5)
        for t in range(3):
            for y in range(4):
                for h in range(2):
                    row = 32 * ((t * 4 + y) * 2 + h)
                    other = raws[t][4 * z + y, quarters[t], :, 256 * h : 256 * h + 256]
                    total = mine[row : row + 32] + jnp.floor(other * scale + 0.5)
                    word = total[:16] + FIELD * total[16:]
                    for x in range(2):
                        outs[t][z, y, 2 * h + x] = word[:, 128 * x : 128 * x + 128]
        return carry

    lax.fori_loop(0, 4, plane, 0)


def levels_for(offset, own, raws, table, tops):
    return pl.pallas_call(
        functools.partial(level_kernel, offset),
        in_specs=[VMEM] * 6,
        out_specs=[VMEM] * 3,
        out_shape=[pltpu.VMEM((4, 4, 4, 16, 128), F32)] * 3,
        compiler_params=pltpu.CompilerParams(vmem_limit_bytes=12 * 2**20),
        cost_estimate=pl.CostEstimate(flops=10**9, bytes_accessed=6 * 10**6, transcendentals=0),
    )(own.reshape(16, 12, 32, 512), *[raw.reshape(16, 4, 32, 512) for raw in raws], table, tops)


def gather_kernel(*refs):
    out = refs[-1]

    def some(i, carry):
        for t in range(3):
            a, b, c, d = (refs[4 * t + k][pl.ds(8 * i, 8)] for k in range(4))
            out[pl.ds(8 * i, 8), 16 * t : 16 * t + 16, :] = (a + b) + (c + d)
        return carry

    lax.fori_loop(0, 8, some, 0)


def sum_four(parts):
    return pl.pallas_call(
        gather_kernel,
        in_specs=[VMEM] * 12,
        out_specs=VMEM,
        out_shape=pltpu.VMEM((64, 48, 128), F32),
        compiler_params=pltpu.CompilerParams(vmem_limit_bytes=12 * 2**20),
        cost_estimate=pl.CostEstimate(flops=10**6, bytes_accessed=8 * 10**6, transcendentals=0),
    )(*[part.reshape(64, 16, 128) for part in parts])


def update_kernel(
    scalars, words_ref, table_ref, sign_ref, weights_ref, first_ref, second_ref, weights_out, first_out, second_out
):
    table = table_ref[...]
    for t in range(3):
        for q in range(4):
            parts = []
            for a in range(4):
                for b in range(4):
                    x, z, y = ((q, a, b), (a, b, q), (a, q, b))[t]
                    parts.append(words_ref[z, y, x, 16 * t : 16 * t + 16, :])
            low = high = jnp.zeros((16, 128), F32)
            for word in parts:
                upper = jnp.floor(word * (1.0 / FIELD) + 0.5)
                high = high + upper
                low = low + (word - upper * FIELD)
            total = jnp.concatenate([low, high], axis=0)
            coarse = jnp.floor(total * (1.0 / 128.0) + 0.5)
            fine = total - coarse * 128.0
            back = 128.0 * jnp.dot(coarse.astype(BF16), table, preferred_element_type=F32) + jnp.dot(
                fine.astype(BF16), table, preferred_element_type=F32
            )
            rows = pl.ds(128 * t + 32 * q, 32)
            grad = (back * scalars[0]) * ROOT * sign_ref[pl.ds(32 * (q % 2), 32), :].astype(F32)
            first = 0.9 * first_ref[rows, :] + 0.1 * grad
            second = 0.95 * second_ref[rows, :] + 0.05 * grad * grad
            weights = weights_ref[rows, :]
            update = (first / scalars[1]) / (jnp.sqrt(second / scalars[2]) + 1e-08) + 0.1 * weights
            weights_out[rows, :] = weights - 0.2 * update
            first_out[rows, :] = first
            second_out[rows, :] = second


def shift(amount):
    return [
        (2 * i + core, 2 * ((i + (amount if core == 0 else -amount)) % 4) + core)
        for i in range(4)
        for core in range(2)
    ]


def shards(gradients, sign_table, loss_scale, step_count, weights, first_moment, second_moment):
    grads = gradients[0, 0]
    table = jnp.asarray(hadamard(BLOCK), BF16)
    twice = jnp.asarray(np.kron(np.eye(2, dtype=np.float32), hadamard(BLOCK)), BF16)
    *raws, own, top_tile = rotate_all(grads, sign_table, twice)
    raws = [lax.ppermute(raw, "core", [(0, 1), (1, 0)]) for raw in raws]
    tops = lax.all_to_all(top_tile, ALL, 0, 0, tiled=True)

    parts = [[] for _ in range(3)]
    for offset in (1, 3, 2, 0):
        outs = levels_for(offset, own, raws, twice, tops)
        for third, out in enumerate(outs):
            parts[third].append(lax.ppermute(out, (FIRST[third], "core"), shift(offset)) if offset else out)
    words = sum_four([part for third in parts for part in third])
    words = lax.all_to_all(words, CHIPS, 0, 0, tiled=True)

    top_value = jnp.max(tops)
    factor = top_value / (127.0 * 128.0 * loss_scale[0])
    steps_float = step_count[0].astype(F32)
    scalars = jnp.stack(
        [
            factor,
            1.0 - jnp.power(F32(0.9), steps_float),
            1.0 - jnp.power(F32(0.95), steps_float),
        ]
    )
    own_signs = lax.dynamic_slice_in_dim(sign_table, lax.axis_index("x") * BLOCK, BLOCK, 1)
    return pl.pallas_call(
        update_kernel,
        in_specs=[pl.BlockSpec(memory_space=pltpu.SMEM)] + [VMEM] * 6,
        out_specs=[VMEM] * 3,
        out_shape=[jax.ShapeDtypeStruct((384, 128), F32)] * 3,
        compiler_params=pltpu.CompilerParams(vmem_limit_bytes=40 * 2**20),
    )(scalars, words.reshape(4, 4, 4, 48, 128), table, own_signs, weights, first_moment, second_moment)


def solution(mesh):
    torus = Mesh(mesh.devices.reshape(4, 4, 4, 2), ("x", "z", "y", "core"))
    owned = P(INTRA, "x")
    return jax.shard_map(
        shards,
        mesh=torus,
        in_specs=(P("x", INTRA, None, None), P(), P(), P(), owned, owned, owned),
        out_specs=(owned, owned, owned),
        check_vma=False,
    )
```

```python
import functools
import math

import jax
import jax.numpy as jnp
import numpy as np
from jax import lax
from jax.experimental import pallas as pl
from jax.experimental.pallas import tpu as pltpu
from jax.sharding import Mesh
from jax.sharding import PartitionSpec as P

BLOCK = 128
SIGN_ROWS = 64
ROOT = 1.0 / math.sqrt(BLOCK)
CHIPS = ("z", "y", "x")
ALL = ("z", "y", "x", "core")
INTRA = ("z", "y", "core")
FIRST = ("x", "y", "z")
FIELD = 4096.0
F32 = jnp.float32
BF16 = jnp.bfloat16


def hadamard(order):
    table = np.ones((1, 1), np.float32)
    while table.shape[0] < order:
        table = np.block([[table, table], [table, -table]])
    return table


def rotate_kernel(grads_ref, sign_ref, table_ref, raw0, raw1, raw2, own_ref, top_ref, buffer, sems):
    core = lax.axis_index("core")
    copies = [pltpu.make_async_copy(grads_ref.at[i], buffer.at[i], sems.at[i]) for i in range(16)]
    for copy in copies:
        copy.start()
    signs = sign_ref[...].astype(F32).astype(BF16)
    table = table_ref[...]

    def fold(value):
        return jnp.max(jnp.abs(value).reshape(-1, 8, 256), axis=0)

    best = jnp.zeros((8, 256), F32)
    for i in range(16):
        copies[i].wait()

        for third, raw_ref in enumerate((raw0, raw1, raw2)):
            rows = pl.ds(128 * third, 128)
            wide = jnp.concatenate([signs, signs], axis=0)
            mine = buffer[i, core, rows, :] * wide
            own_ref[i, rows, :] = mine
            other = buffer[i, 1 - core, rows, :] * wide
            block = jnp.concatenate([v[:, 256 * h : 256 * h + 256] for v in (other, mine) for h in range(2)], axis=0)
            turned = jnp.dot(block, table, preferred_element_type=F32) * ROOT
            raw_ref[i, :, :256] = turned[:128]
            raw_ref[i, :, 256:] = turned[128:256]
            best = jnp.maximum(best, fold(turned))
    top_ref[...] = jnp.broadcast_to(jnp.max(best, axis=(0, 1), keepdims=True), (128, 128))


VMEM = pl.BlockSpec(memory_space=pltpu.VMEM)


def rotate_all(grads, signs, table):
    return pl.pallas_call(
        rotate_kernel,
        in_specs=[pl.BlockSpec(memory_space=pl.ANY), VMEM, VMEM],
        out_specs=[VMEM] * 5,
        out_shape=[pltpu.VMEM((16, 128, 512), F32)] * 3
        + [
            pltpu.VMEM((16, 384, 512), BF16),
            jax.ShapeDtypeStruct((128, 128), F32),
        ],
        scratch_shapes=[pltpu.VMEM((16, 2, 384, 512), BF16), pltpu.SemaphoreType.DMA((16,))],
        compiler_params=pltpu.CompilerParams(vmem_limit_bytes=40 * 2**20),
        cost_estimate=pl.CostEstimate(flops=6 * 10**9, bytes_accessed=12 * 10**6, transcendentals=0),
    )(grads.reshape(16, 2, 384, 512), signs, table)


def nearest(value, unit):
    return jnp.floor(value * (1.0 / unit) + 0.5)


def pack_eight(v):
    last = v[6] + 512.0 * v[7]
    high = nearest(last, 4096.0)
    rest = last - 4096.0 * high
    middle = nearest(rest, 64.0)
    thirds = (high, middle, rest - 64.0 * middle)
    return [(v[2 * i] + 512.0 * v[2 * i + 1]) + 262144.0 * thirds[i] for i in range(3)]


def unpack_eight(words):
    thirds = [nearest(word, 262144.0) for word in words]
    last = (thirds[0] * 4096.0 + thirds[1] * 64.0) + thirds[2]
    values = []
    for pair in [word - 262144.0 * third for word, third in zip(words, thirds)] + [last]:
        upper = nearest(pair, 512.0)
        values += [pair - 512.0 * upper, upper]
    return values


def level_kernel(offset, own_ref, raw0, raw1, raw2, table_ref, top_ref, *outs):
    table = table_ref[...]
    scale = 127.0 / jnp.max(top_ref[...], axis=(0, 1), keepdims=True)
    ahead = jnp.where(lax.axis_index("core") == 0, offset, (4 - offset) % 4)
    quarters = [lax.rem(lax.axis_index(axis) + ahead, 4) for axis in FIRST]
    raws = (raw0, raw1, raw2)

    def plane(z, carry):
        blocks = [own_ref[4 * z + y, 4 * t + quarters[t]] for t in range(3) for y in range(4)]
        stacked = jnp.concatenate([v[:, 256 * h : 256 * h + 256] for v in blocks for h in range(2)], axis=0)
        mine = jnp.dot(stacked, table, preferred_element_type=F32) * ROOT
        mine = jnp.floor(mine * scale + 0.5)
        for t in range(3):
            for pair in range(2):
                for h in range(2):
                    groups = []
                    for y in (2 * pair, 2 * pair + 1):
                        row = 32 * ((t * 4 + y) * 2 + h)
                        other = raws[t][4 * z + y, quarters[t], :, 256 * h : 256 * h + 256]
                        total = mine[row : row + 32] + jnp.floor(other * scale + 0.5)
                        groups += [total[8 * g : 8 * g + 8] for g in range(4)]
                    if offset:
                        for i, word in enumerate(pack_eight(groups)):
                            outs[t][z, pair, i, :, 256 * h : 256 * h + 256] = word
                        continue
                    for k in range(2):
                        low, lower, high, higher = groups[4 * k : 4 * k + 4]
                        word = jnp.concatenate([low + FIELD * high, lower + FIELD * higher], axis=0)
                        for x in range(2):
                            place = outs[0].at[z, 2 * pair + k, 2 * h + x, 16 * t : 16 * t + 16, :]
                            place[...] = word[:, 128 * x : 128 * x + 128]
        return carry

    lax.fori_loop(0, 4, plane, 0)


def levels_for(offset, own, raws, table, tops):
    shapes = [(4, 2, 3, 8, 512)] * 3 if offset else [(4, 4, 4, 48, 128)]
    return pl.pallas_call(
        functools.partial(level_kernel, offset),
        in_specs=[VMEM] * 6,
        out_specs=[VMEM] * len(shapes),
        out_shape=[pltpu.VMEM(shape, F32) for shape in shapes],
        compiler_params=pltpu.CompilerParams(vmem_limit_bytes=12 * 2**20),
        cost_estimate=pl.CostEstimate(flops=10**9, bytes_accessed=6 * 10**6, transcendentals=0),
    )(own.reshape(16, 12, 32, 512), *[raw.reshape(16, 4, 32, 512) for raw in raws], table, tops)


def add_kernel(sums_ref, part0, part1, part2, out_ref):
    def plane(z, carry):
        for t, part in enumerate((part0, part1, part2)):
            for pair in range(2):
                v = unpack_eight([part[z, pair, i] for i in range(3)])
                for k in range(2):
                    low, lower, high, higher = v[4 * k : 4 * k + 4]
                    for j, word in enumerate((low + FIELD * high, lower + FIELD * higher)):
                        for x in range(4):
                            where = (z, 2 * pair + k, x, pl.ds(16 * t + 8 * j, 8))
                            out_ref[where] = sums_ref[where] + word[:, 128 * x : 128 * x + 128]
        return carry

    lax.fori_loop(0, 4, plane, 0)


def add_parts(sums, parts):
    return pl.pallas_call(
        add_kernel,
        in_specs=[VMEM] * 4,
        out_specs=VMEM,
        out_shape=pltpu.VMEM((4, 4, 4, 48, 128), F32),
        compiler_params=pltpu.CompilerParams(vmem_limit_bytes=12 * 2**20),
        cost_estimate=pl.CostEstimate(flops=10**7, bytes_accessed=4 * 10**6, transcendentals=0),
    )(sums, *parts)


def update_kernel(
    scalars, words_ref, table_ref, sign_ref, weights_ref, first_ref, second_ref, weights_out, first_out, second_out
):
    table = table_ref[...]
    for t in range(3):
        for q in range(4):
            parts = []
            for a in range(4):
                for b in range(4):
                    x, z, y = ((q, a, b), (a, b, q), (a, q, b))[t]
                    parts.append(words_ref[z, y, x, 16 * t : 16 * t + 16, :])
            low = high = jnp.zeros((16, 128), F32)
            for word in parts:
                upper = jnp.floor(word * (1.0 / FIELD) + 0.5)
                high = high + upper
                low = low + (word - upper * FIELD)
            total = jnp.concatenate([low, high], axis=0)
            coarse = jnp.floor(total * (1.0 / 128.0) + 0.5)
            fine = total - coarse * 128.0
            back = 128.0 * jnp.dot(coarse.astype(BF16), table, preferred_element_type=F32) + jnp.dot(
                fine.astype(BF16), table, preferred_element_type=F32
            )
            rows = pl.ds(128 * t + 32 * q, 32)
            grad = (back * scalars[0]) * ROOT * sign_ref[pl.ds(32 * (q % 2), 32), :].astype(F32)
            first = 0.9 * first_ref[rows, :] + 0.1 * grad
            second = 0.95 * second_ref[rows, :] + 0.05 * grad * grad
            weights = weights_ref[rows, :]
            update = (first / scalars[1]) / (jnp.sqrt(second / scalars[2]) + 1e-08) + 0.1 * weights
            weights_out[rows, :] = weights - 0.2 * update
            first_out[rows, :] = first
            second_out[rows, :] = second


def shift(amount):
    return [
        (2 * i + core, 2 * ((i + (amount if core == 0 else -amount)) % 4) + core)
        for i in range(4)
        for core in range(2)
    ]


def shards(gradients, sign_table, loss_scale, step_count, weights, first_moment, second_moment):
    grads = gradients[0, 0]
    table = jnp.asarray(hadamard(BLOCK), BF16)
    twice = jnp.asarray(np.kron(np.eye(2, dtype=np.float32), hadamard(BLOCK)), BF16)
    *raws, own, top_tile = rotate_all(grads, sign_table, twice)
    raws = [lax.ppermute(raw, "core", [(0, 1), (1, 0)]) for raw in raws]
    tops = lax.all_to_all(top_tile, ALL, 0, 0, tiled=True)

    arrived = []
    for offset in (1, 3, 2):
        outs = levels_for(offset, own, raws, twice, tops)
        arrived.append([lax.ppermute(out, (axis, "core"), shift(offset)) for out, axis in zip(outs, FIRST)])
    (words,) = levels_for(0, own, raws, twice, tops)
    for parts in arrived:
        words = add_parts(words, parts)
    words = words.reshape(64, 48, 128)
    words = lax.all_to_all(words, CHIPS, 0, 0, tiled=True)

    top_value = jnp.max(tops)
    factor = top_value / (127.0 * 128.0 * loss_scale[0])
    steps_float = step_count[0].astype(F32)
    scalars = jnp.stack(
        [
            factor,
            1.0 - jnp.power(F32(0.9), steps_float),
            1.0 - jnp.power(F32(0.95), steps_float),
        ]
    )
    own_signs = lax.dynamic_slice_in_dim(sign_table, lax.axis_index("x") * BLOCK, BLOCK, 1)
    return pl.pallas_call(
        update_kernel,
        in_specs=[pl.BlockSpec(memory_space=pltpu.SMEM)] + [VMEM] * 6,
        out_specs=[VMEM] * 3,
        out_shape=[jax.ShapeDtypeStruct((384, 128), F32)] * 3,
        compiler_params=pltpu.CompilerParams(vmem_limit_bytes=40 * 2**20),
    )(scalars, words.reshape(4, 4, 4, 48, 128), table, own_signs, weights, first_moment, second_moment)


def solution(mesh):
    torus = Mesh(mesh.devices.reshape(4, 4, 4, 2), ("x", "z", "y", "core"))
    owned = P(INTRA, "x")
    return jax.shard_map(
        shards,
        mesh=torus,
        in_specs=(P("x", INTRA, None, None), P(), P(), P(), owned, owned, owned),
        out_specs=(owned, owned, owned),
        check_vma=False,
    )
```

```python
import functools
import math

import jax
import jax.numpy as jnp
import numpy as np
from jax import lax
from jax.experimental import pallas as pl
from jax.experimental.pallas import tpu as pltpu
from jax.sharding import Mesh
from jax.sharding import PartitionSpec as P

BLOCK = 128
SIGN_ROWS = 64
ROOT = 1.0 / math.sqrt(BLOCK)
CHIPS = ("z", "y", "x")
ALL = ("z", "y", "x", "core")
INTRA = ("z", "y", "core")
MESH = ("x", "z", "y", "core")
FIELD = 4096.0
F32 = jnp.float32
BF16 = jnp.bfloat16


def hadamard(order):
    table = np.ones((1, 1), np.float32)
    while table.shape[0] < order:
        table = np.block([[table, table], [table, -table]])
    return table


def rotate_kernel(grads_ref, sign_ref, table_ref, raw0, raw1, raw2, own_ref, top_ref, buffer, sems):
    core = lax.axis_index("core")
    copies = [pltpu.make_async_copy(grads_ref.at[i], buffer.at[i], sems.at[i]) for i in range(16)]
    for copy in copies:
        copy.start()
    signs = sign_ref[...].astype(F32).astype(BF16)
    table = table_ref[...]

    def fold(value):
        return jnp.max(jnp.abs(value).reshape(-1, 8, 256), axis=0)

    best = jnp.zeros((8, 256), F32)
    for i in range(16):
        copies[i].wait()

        for third, raw_ref in enumerate((raw0, raw1, raw2)):
            rows = pl.ds(128 * third, 128)
            wide = jnp.concatenate([signs, signs], axis=0)
            mine = buffer[i, core, rows, :] * wide
            own_ref[i, rows, :] = mine
            other = buffer[i, 1 - core, rows, :] * wide
            for v, keep in ((other, True), (mine, False)):
                block = jnp.concatenate([v[:, :256], v[:, 256:]], axis=0)
                turned = jnp.dot(block, table, preferred_element_type=F32)
                if keep:
                    raw_ref[i, :, :256] = turned[:128] * ROOT
                    raw_ref[i, :, 256:] = turned[128:] * ROOT
                best = jnp.maximum(best, fold(turned))
    top_ref[...] = jnp.broadcast_to(jnp.max(best, axis=(0, 1), keepdims=True) * ROOT, (128, 128))


VMEM = pl.BlockSpec(memory_space=pltpu.VMEM)


def rotate_all(grads, signs, table):
    return pl.pallas_call(
        rotate_kernel,
        in_specs=[pl.BlockSpec(memory_space=pl.ANY), VMEM, VMEM],
        out_specs=[VMEM] * 5,
        out_shape=[pltpu.VMEM((16, 128, 512), F32)] * 3
        + [
            pltpu.VMEM((16, 384, 512), BF16),
            jax.ShapeDtypeStruct((128, 128), F32),
        ],
        scratch_shapes=[pltpu.VMEM((16, 2, 384, 512), BF16), pltpu.SemaphoreType.DMA((16,))],
        compiler_params=pltpu.CompilerParams(vmem_limit_bytes=40 * 2**20),
        cost_estimate=pl.CostEstimate(flops=6 * 10**9, bytes_accessed=12 * 10**6, transcendentals=0),
    )(grads.reshape(16, 2, 384, 512), signs, table)


def nearest(value, unit):
    return jnp.floor(value * (1.0 / unit) + 0.5)


def pack_eight(v):
    last = v[6] + 512.0 * v[7]
    high = nearest(last, 4096.0)
    rest = last - 4096.0 * high
    middle = nearest(rest, 64.0)
    thirds = (high, middle, rest - 64.0 * middle)
    return [(v[2 * i] + 512.0 * v[2 * i + 1]) + 262144.0 * thirds[i] for i in range(3)]


def unpack_eight(words):
    thirds = [nearest(word, 262144.0) for word in words]
    last = (thirds[0] * 4096.0 + thirds[1] * 64.0) + thirds[2]
    values = []
    for pair in [word - 262144.0 * third for word, third in zip(words, thirds)] + [last]:
        upper = nearest(pair, 512.0)
        values += [pair - 512.0 * upper, upper]
    return values


def level_kernel(offset, own_ref, raw0, raw1, raw2, table_ref, top_ref, *outs):
    table = table_ref[...]
    scale = 127.0 / jnp.max(top_ref[...], axis=(0, 1), keepdims=True)
    even = lax.axis_index("core") == 0
    flat = lax.rem(jnp.where(even, lax.axis_index("x"), lax.axis_index("y")) + offset, 4)
    ahead = jnp.where(even, offset, (4 - offset) % 4)
    quarters = [flat, flat, lax.rem(lax.axis_index("z") + ahead, 4)]
    raws = (raw0, raw1, raw2)

    def plane(z, carry):
        blocks = [own_ref[4 * z + y, 4 * t + quarters[t]] for t in range(3) for y in range(4)]
        stacked = jnp.concatenate([v[:, 256 * h : 256 * h + 256] for v in blocks for h in range(2)], axis=0)
        mine = jnp.dot(stacked, table, preferred_element_type=F32) * ROOT
        mine = jnp.floor(mine * scale + 0.5)
        for t in range(3):
            for pair in range(2):
                for h in range(2):
                    groups = []
                    for y in (2 * pair, 2 * pair + 1):
                        row = 32 * ((t * 4 + y) * 2 + h)
                        other = raws[t][4 * z + y, quarters[t], :, 256 * h : 256 * h + 256]
                        total = mine[row : row + 32] + jnp.floor(other * scale + 0.5)
                        groups += [total[8 * g : 8 * g + 8] for g in range(4)]
                    if offset:
                        for i, word in enumerate(pack_eight(groups)):
                            cols = slice(256 * h, 256 * h + 256)
                            if t < 2:
                                outs[0][t, z, pair, i, :, cols] = word
                            else:
                                outs[1][z, pair, i, :, cols] = word
                        continue
                    for k in range(2):
                        low, lower, high, higher = groups[4 * k : 4 * k + 4]
                        word = jnp.concatenate([low + FIELD * high, lower + FIELD * higher], axis=0)
                        for x in range(2):
                            place = outs[0].at[z, 2 * pair + k, 2 * h + x, 16 * t : 16 * t + 16, :]
                            place[...] = word[:, 128 * x : 128 * x + 128]
        return carry

    lax.fori_loop(0, 4, plane, 0)


def levels_for(offset, own, raws, table, tops):
    shapes = [(2, 4, 2, 3, 8, 512), (4, 2, 3, 8, 512)] if offset else [(4, 4, 4, 48, 128)]
    return pl.pallas_call(
        functools.partial(level_kernel, offset),
        in_specs=[VMEM] * 6,
        out_specs=[VMEM] * len(shapes),
        out_shape=[pltpu.VMEM(shape, F32) for shape in shapes],
        compiler_params=pltpu.CompilerParams(vmem_limit_bytes=12 * 2**20),
        cost_estimate=pl.CostEstimate(flops=10**6, bytes_accessed=10**4, transcendentals=0),
    )(own.reshape(16, 12, 32, 512), *[raw.reshape(16, 4, 32, 512) for raw in raws], table, tops)


def add_kernel(sums_ref, flat_ref, tall_ref, out_ref):
    def plane(z, carry):
        for t, part in enumerate((flat_ref.at[0], flat_ref.at[1], tall_ref)):
            for pair in range(2):
                v = unpack_eight([part[z, pair, i] for i in range(3)])
                for k in range(2):
                    low, lower, high, higher = v[4 * k : 4 * k + 4]
                    for j, word in enumerate((low + FIELD * high, lower + FIELD * higher)):
                        for x in range(4):
                            where = (z, 2 * pair + k, x, pl.ds(16 * t + 8 * j, 8))
                            out_ref[where] = sums_ref[where] + word[:, 128 * x : 128 * x + 128]
        return carry

    lax.fori_loop(0, 4, plane, 0)


def add_parts(sums, parts):
    return pl.pallas_call(
        add_kernel,
        in_specs=[VMEM] * 3,
        out_specs=VMEM,
        out_shape=pltpu.VMEM((4, 4, 4, 48, 128), F32),
        compiler_params=pltpu.CompilerParams(vmem_limit_bytes=12 * 2**20),
        cost_estimate=pl.CostEstimate(flops=10**7, bytes_accessed=4 * 10**6, transcendentals=0),
    )(sums, *parts)


def update_kernel(
    scalars, words_ref, table_ref, sign_ref, weights_ref, first_ref, second_ref, weights_out, first_out, second_out
):
    table = table_ref[...]
    even = lax.axis_index("core") == 0
    for t in range(3):
        for q in range(4):
            parts = []
            for a in range(4):
                for b in range(4):
                    z, y, x = (a, jnp.where(even, b, q), jnp.where(even, q, b)) if t < 2 else (q, a, b)
                    parts.append(words_ref[z, y, x, 16 * t : 16 * t + 16, :])
            low = high = jnp.zeros((16, 128), F32)
            for word in parts:
                upper = jnp.floor(word * (1.0 / FIELD) + 0.5)
                high = high + upper
                low = low + (word - upper * FIELD)
            total = jnp.concatenate([low, high], axis=0)
            coarse = jnp.floor(total * (1.0 / 128.0) + 0.5)
            fine = total - coarse * 128.0
            back = 128.0 * jnp.dot(coarse.astype(BF16), table, preferred_element_type=F32) + jnp.dot(
                fine.astype(BF16), table, preferred_element_type=F32
            )
            rows = pl.ds(128 * t + 32 * q, 32)
            grad = (back * scalars[0]) * ROOT * sign_ref[pl.ds(32 * (q % 2), 32), :].astype(F32)
            first = 0.9 * first_ref[rows, :] + 0.1 * grad
            second = 0.95 * second_ref[rows, :] + 0.05 * grad * grad
            weights = weights_ref[rows, :]
            update = (first / scalars[1]) / (jnp.sqrt(second / scalars[2]) + 1e-08) + 0.1 * weights
            weights_out[rows, :] = weights - 0.2 * update
            first_out[rows, :] = first
            second_out[rows, :] = second


def shift_flat(amount):
    index = np.arange(128).reshape(4, 4, 4, 2)
    ahead = np.stack([np.roll(index[..., 0], -amount, axis=0), np.roll(index[..., 1], -amount, axis=2)], axis=-1)
    return [(int(source), int(target)) for source, target in zip(index.ravel(), ahead.ravel())]


def shift_tall(amount):
    return [
        (2 * i + core, 2 * ((i + (amount if core == 0 else -amount)) % 4) + core)
        for i in range(4)
        for core in range(2)
    ]


def shards(gradients, sign_table, loss_scale, step_count, weights, first_moment, second_moment):
    grads = gradients[0, 0]
    table = jnp.asarray(hadamard(BLOCK), BF16)
    twice = jnp.asarray(np.kron(np.eye(2, dtype=np.float32), hadamard(BLOCK)), BF16)
    *raws, own, top_tile = rotate_all(grads, sign_table, twice)
    raws = [lax.ppermute(raw, "core", [(0, 1), (1, 0)]) for raw in raws]
    tops = lax.all_to_all(top_tile, ALL, 0, 0, tiled=True)

    arrived = []
    for offset in (1, 3, 2):
        flat, tall = levels_for(offset, own, raws, twice, tops)
        flat = lax.ppermute(flat, MESH, shift_flat(offset))
        arrived.append((flat, lax.ppermute(tall, ("z", "core"), shift_tall(offset))))
    (words,) = levels_for(0, own, raws, twice, tops)
    for parts in arrived:
        words = add_parts(words, parts)
    words = words.reshape(64, 48, 128)
    words = lax.all_to_all(words, CHIPS, 0, 0, tiled=True)

    top_value = jnp.max(tops)
    factor = top_value / (127.0 * 128.0 * loss_scale[0])
    steps_float = step_count[0].astype(F32)
    scalars = jnp.stack(
        [
            factor,
            1.0 - jnp.power(F32(0.9), steps_float),
            1.0 - jnp.power(F32(0.95), steps_float),
        ]
    )
    own_signs = lax.dynamic_slice_in_dim(sign_table, lax.axis_index("x") * BLOCK, BLOCK, 1)
    return pl.pallas_call(
        update_kernel,
        in_specs=[pl.BlockSpec(memory_space=pltpu.SMEM)] + [VMEM] * 6,
        out_specs=[VMEM] * 3,
        out_shape=[jax.ShapeDtypeStruct((384, 128), F32)] * 3,
        compiler_params=pltpu.CompilerParams(vmem_limit_bytes=40 * 2**20),
    )(scalars, words.reshape(4, 4, 4, 48, 128), table, own_signs, weights, first_moment, second_moment)


def solution(mesh):
    torus = Mesh(mesh.devices.reshape(4, 4, 4, 2), ("x", "z", "y", "core"))
    owned = P(INTRA, "x")
    return jax.shard_map(
        shards,
        mesh=torus,
        in_specs=(P("x", INTRA, None, None), P(), P(), P(), owned, owned, owned),
        out_specs=(owned, owned, owned),
        check_vma=False,
    )
```

```python
import functools
import math

import jax
import jax.numpy as jnp
import numpy as np
from jax import lax
from jax.experimental import pallas as pl
from jax.experimental.pallas import tpu as pltpu
from jax.sharding import Mesh
from jax.sharding import PartitionSpec as P

BLOCK = 128
SIGN_ROWS = 64
ROOT = 1.0 / math.sqrt(BLOCK)
CHIPS = ("z", "y", "x")
ALL = ("z", "y", "x", "core")
INTRA = ("z", "y", "core")
MESH = ("x", "z", "y", "core")
FIELD = 4096.0
F32 = jnp.float32
BF16 = jnp.bfloat16


def hadamard(order):
    table = np.ones((1, 1), np.float32)
    while table.shape[0] < order:
        table = np.block([[table, table], [table, -table]])
    return table


def rotate_kernel(grads_ref, sign_ref, table_ref, raw0, raw1, raw2, own_ref, top_ref, buffer, sems):
    core = lax.axis_index("core")
    copies = [pltpu.make_async_copy(grads_ref.at[i], buffer.at[i], sems.at[i]) for i in range(16)]
    for copy in copies:
        copy.start()
    signs = sign_ref[...].astype(F32).astype(BF16)
    table = table_ref[...]

    def fold(value):
        return jnp.max(jnp.abs(value).reshape(-1, 8, 256), axis=0)

    best = jnp.zeros((8, 256), F32)
    for i in range(16):
        copies[i].wait()

        for third, raw_ref in enumerate((raw0, raw1, raw2)):
            rows = pl.ds(128 * third, 128)
            wide = jnp.concatenate([signs, signs], axis=0)
            mine = buffer[i, core, rows, :] * wide
            own_ref[i, rows, :] = mine
            other = buffer[i, 1 - core, rows, :] * wide
            for v, keep in ((other, True), (mine, False)):
                block = jnp.concatenate([v[:, :256], v[:, 256:]], axis=0)
                turned = jnp.dot(block, table, preferred_element_type=F32)
                if keep:
                    raw_ref[i, :, :256] = turned[:128] * ROOT
                    raw_ref[i, :, 256:] = turned[128:] * ROOT
                best = jnp.maximum(best, fold(turned))
    top_ref[...] = jnp.broadcast_to(jnp.max(best, axis=(0, 1), keepdims=True) * ROOT, (128, 128))


VMEM = pl.BlockSpec(memory_space=pltpu.VMEM)


def rotate_all(grads, signs, table):
    return pl.pallas_call(
        rotate_kernel,
        in_specs=[pl.BlockSpec(memory_space=pl.ANY), VMEM, VMEM],
        out_specs=[VMEM] * 5,
        out_shape=[pltpu.VMEM((16, 128, 512), F32)] * 3
        + [
            pltpu.VMEM((16, 384, 512), BF16),
            jax.ShapeDtypeStruct((128, 128), F32),
        ],
        scratch_shapes=[pltpu.VMEM((16, 2, 384, 512), BF16), pltpu.SemaphoreType.DMA((16,))],
        compiler_params=pltpu.CompilerParams(vmem_limit_bytes=40 * 2**20),
        cost_estimate=pl.CostEstimate(flops=6 * 10**9, bytes_accessed=12 * 10**6, transcendentals=0),
    )(grads.reshape(16, 2, 384, 512), signs, table)


def nearest(value, unit):
    return jnp.floor(value * (1.0 / unit) + 0.5)


def pack_eight(v):
    last = v[6] + 512.0 * v[7]
    high = nearest(last, 4096.0)
    rest = last - 4096.0 * high
    middle = nearest(rest, 64.0)
    thirds = (high, middle, rest - 64.0 * middle)
    return [(v[2 * i] + 512.0 * v[2 * i + 1]) + 262144.0 * thirds[i] for i in range(3)]


def unpack_eight(words):
    thirds = [nearest(word, 262144.0) for word in words]
    last = (thirds[0] * 4096.0 + thirds[1] * 64.0) + thirds[2]
    values = []
    for pair in [word - 262144.0 * third for word, third in zip(words, thirds)] + [last]:
        upper = nearest(pair, 512.0)
        values += [pair - 512.0 * upper, upper]
    return values


def level_kernel(offset, own_ref, raw0, raw1, raw2, table_ref, top_ref, *outs):
    table = table_ref[...]
    scale = 127.0 / jnp.max(top_ref[...], axis=(0, 1), keepdims=True)
    even = lax.axis_index("core") == 0
    flat = lax.rem(jnp.where(even, lax.axis_index("x"), lax.axis_index("y")) + offset, 4)
    ahead = jnp.where(even, offset, (4 - offset) % 4)
    quarters = [flat, flat, lax.rem(lax.axis_index("z") + ahead, 4)]
    raws = (raw0, raw1, raw2)

    def plane(z, carry):
        blocks = [own_ref[4 * z + y, 4 * t + quarters[t]] for t in range(3) for y in range(4)]
        stacked = jnp.concatenate([v[:, 256 * h : 256 * h + 256] for v in blocks for h in range(2)], axis=0)
        mine = jnp.dot(stacked, table, preferred_element_type=F32) * ROOT
        mine = jnp.floor(mine * scale + 0.5)
        for t in range(3):
            for pair in range(2):
                for h in range(2):
                    groups = []
                    for y in (2 * pair, 2 * pair + 1):
                        row = 32 * ((t * 4 + y) * 2 + h)
                        other = raws[t][4 * z + y, quarters[t], :, 256 * h : 256 * h + 256]
                        total = mine[row : row + 32] + jnp.floor(other * scale + 0.5)
                        groups += [total[8 * g : 8 * g + 8] for g in range(4)]
                    if offset:
                        for i, word in enumerate(pack_eight(groups)):
                            cols = slice(256 * h, 256 * h + 256)
                            if t < 2:
                                outs[0][t, z, pair, i, :, cols] = word
                            else:
                                outs[1][z, pair, i, :, cols] = word
                        continue
                    for k in range(2):
                        low, lower, high, higher = groups[4 * k : 4 * k + 4]
                        word = jnp.concatenate([low + FIELD * high, lower + FIELD * higher], axis=0)
                        for x in range(2):
                            place = outs[0].at[z, 2 * pair + k, 2 * h + x, 16 * t : 16 * t + 16, :]
                            place[...] = word[:, 128 * x : 128 * x + 128]
        return carry

    lax.fori_loop(0, 4, plane, 0)


def levels_for(offset, own, raws, table, tops):
    shapes = [(2, 4, 2, 3, 8, 512), (4, 2, 3, 8, 512)] if offset else [(4, 4, 4, 48, 128)]
    return pl.pallas_call(
        functools.partial(level_kernel, offset),
        in_specs=[VMEM] * 6,
        out_specs=[VMEM] * len(shapes),
        out_shape=[pltpu.VMEM(shape, F32) for shape in shapes],
        compiler_params=pltpu.CompilerParams(vmem_limit_bytes=12 * 2**20),
        cost_estimate=pl.CostEstimate(flops=10**6, bytes_accessed=10**4, transcendentals=0),
    )(own.reshape(16, 12, 32, 512), *[raw.reshape(16, 4, 32, 512) for raw in raws], table, tops)


def add_plane(z, sums_ref, parts, out_ref):
    for t, part in enumerate(parts):
        for pair in range(2):
            v = unpack_eight([part[z, pair, i] for i in range(3)])
            for k in range(2):
                low, lower, high, higher = v[4 * k : 4 * k + 4]
                for j, word in enumerate((low + FIELD * high, lower + FIELD * higher)):
                    for x in range(4):
                        where = (z, 2 * pair + k, x, pl.ds(16 * t + 8 * j, 8))
                        out_ref[where] = sums_ref[where] + word[:, 128 * x : 128 * x + 128]


def add_kernel(sums_ref, flat_ref, tall_ref, out_ref):
    parts = (flat_ref.at[0], flat_ref.at[1], tall_ref)

    def plane(z, carry):
        add_plane(z, sums_ref, parts, out_ref)
        return carry

    lax.fori_loop(0, 4, plane, 0)


def last_add_kernel(sums_ref, flat_ref, tall_ref, out_ref, buffer, sems):
    parts = (flat_ref.at[0], flat_ref.at[1], tall_ref)
    copies = [pltpu.make_async_copy(buffer.at[z], out_ref.at[z], sems.at[z]) for z in range(4)]
    for z in range(4):
        add_plane(z, sums_ref, parts, buffer)
        copies[z].start()
    for copy in copies:
        copy.wait()


def add_parts(sums, parts, last):
    shape = (4, 4, 4, 48, 128)
    return pl.pallas_call(
        last_add_kernel if last else add_kernel,
        in_specs=[VMEM] * 3,
        out_specs=pl.BlockSpec(memory_space=pl.ANY) if last else VMEM,
        out_shape=jax.ShapeDtypeStruct(shape, F32) if last else pltpu.VMEM(shape, F32),
        scratch_shapes=[pltpu.VMEM(shape, F32), pltpu.SemaphoreType.DMA((4,))] if last else [],
        compiler_params=pltpu.CompilerParams(vmem_limit_bytes=12 * 2**20),
        cost_estimate=pl.CostEstimate(flops=10**7, bytes_accessed=4 * 10**6, transcendentals=0),
    )(sums, *parts)


def update_kernel(
    scalars, words_ref, table_ref, sign_ref, weights_ref, first_ref, second_ref, weights_out, first_out, second_out
):
    table = table_ref[...]
    even = lax.axis_index("core") == 0
    coarse, fine = [], []
    for t in range(3):
        for q in range(4):
            low = high = jnp.zeros((16, 128), F32)
            for a in range(4):
                for b in range(4):
                    z, y, x = (a, jnp.where(even, b, q), jnp.where(even, q, b)) if t < 2 else (q, a, b)
                    word = words_ref[z, y, x, 16 * t : 16 * t + 16, :]
                    upper = nearest(word, FIELD)
                    high = high + upper
                    low = low + (word - upper * FIELD)
            total = jnp.concatenate([low, high], axis=0)
            coarse.append(nearest(total, 128.0))
            fine.append(total - coarse[-1] * 128.0)
    digits = jnp.concatenate(coarse + fine, axis=0).astype(BF16)
    turned = jnp.dot(digits, table, preferred_element_type=F32)
    signs = jnp.concatenate([sign_ref[...].astype(F32)] * 6, axis=0)
    grad = ((128.0 * turned[:384] + turned[384:]) * scalars[0]) * ROOT * signs
    first = 0.9 * first_ref[...] + 0.1 * grad
    second = 0.95 * second_ref[...] + 0.05 * grad * grad
    weights = weights_ref[...]
    update = (first / scalars[1]) / (jnp.sqrt(second / scalars[2]) + 1e-08) + 0.1 * weights
    weights_out[...] = weights - 0.2 * update
    first_out[...] = first
    second_out[...] = second


def shift_flat(amount):
    index = np.arange(128).reshape(4, 4, 4, 2)
    ahead = np.stack([np.roll(index[..., 0], -amount, axis=0), np.roll(index[..., 1], -amount, axis=2)], axis=-1)
    return [(int(source), int(target)) for source, target in zip(index.ravel(), ahead.ravel())]


def shift_tall(amount):
    return [
        (2 * i + core, 2 * ((i + (amount if core == 0 else -amount)) % 4) + core)
        for i in range(4)
        for core in range(2)
    ]


def shards(gradients, sign_table, loss_scale, step_count, weights, first_moment, second_moment):
    grads = gradients[0, 0]
    table = jnp.asarray(hadamard(BLOCK), BF16)
    twice = jnp.asarray(np.kron(np.eye(2, dtype=np.float32), hadamard(BLOCK)), BF16)
    *raws, own, top_tile = rotate_all(grads, sign_table, twice)
    raws = [lax.ppermute(raw, "core", [(0, 1), (1, 0)]) for raw in raws]
    tops = lax.all_to_all(top_tile, ALL, 0, 0, tiled=True)

    arrived = []
    for offset in (1, 3, 2):
        flat, tall = levels_for(offset, own, raws, twice, tops)
        flat = lax.ppermute(flat, MESH, shift_flat(offset))
        arrived.append((flat, lax.ppermute(tall, ("z", "core"), shift_tall(offset))))
    (words,) = levels_for(0, own, raws, twice, tops)
    for number, parts in enumerate(arrived):
        words = add_parts(words, parts, number == 2)
    words = words.reshape(64, 48, 128)
    words = lax.all_to_all(words, CHIPS, 0, 0, tiled=True)

    top_value = jnp.max(tops)
    factor = top_value / (127.0 * 128.0 * loss_scale[0])
    steps_float = step_count[0].astype(F32)
    scalars = jnp.stack(
        [
            factor,
            1.0 - jnp.power(F32(0.9), steps_float),
            1.0 - jnp.power(F32(0.95), steps_float),
        ]
    )
    own_signs = lax.dynamic_slice_in_dim(sign_table, lax.axis_index("x") * BLOCK, BLOCK, 1)
    return pl.pallas_call(
        update_kernel,
        in_specs=[pl.BlockSpec(memory_space=pltpu.SMEM)] + [VMEM] * 6,
        out_specs=[VMEM] * 3,
        out_shape=[jax.ShapeDtypeStruct((384, 128), F32)] * 3,
        compiler_params=pltpu.CompilerParams(vmem_limit_bytes=40 * 2**20),
    )(scalars, words.reshape(4, 4, 4, 48, 128), table, own_signs, weights, first_moment, second_moment)


def solution(mesh):
    torus = Mesh(mesh.devices.reshape(4, 4, 4, 2), ("x", "z", "y", "core"))
    owned = P(INTRA, "x")
    return jax.shard_map(
        shards,
        mesh=torus,
        in_specs=(P("x", INTRA, None, None), P(), P(), P(), owned, owned, owned),
        out_specs=(owned, owned, owned),
        check_vma=False,
    )
```

```python
import functools
import math

import jax
import jax.numpy as jnp
import numpy as np
from jax import lax
from jax.experimental import pallas as pl
from jax.experimental.pallas import tpu as pltpu
from jax.sharding import Mesh
from jax.sharding import PartitionSpec as P

BLOCK = 128
SIGN_ROWS = 64
ROOT = 1.0 / math.sqrt(BLOCK)
CHIPS = ("z", "y", "x")
ALL = ("z", "y", "x", "core")
INTRA = ("z", "y", "core")
MESH = ("x", "z", "y", "core")
FIELD = 4096.0
F32 = jnp.float32
BF16 = jnp.bfloat16


def hadamard(order):
    table = np.ones((1, 1), np.float32)
    while table.shape[0] < order:
        table = np.block([[table, table], [table, -table]])
    return table


def rotate_kernel(start, grads_ref, sign_ref, table_ref, raw_ref, own_ref, top_ref, buffer, sems):
    core = lax.axis_index("core")
    copies = [pltpu.make_async_copy(grads_ref.at[start + i], buffer.at[i], sems.at[i]) for i in range(8)]
    for copy in copies:
        copy.start()
    signs = sign_ref[...].astype(F32).astype(BF16)
    table = table_ref[...]

    def fold(value):
        return jnp.max(jnp.abs(value).reshape(-1, 8, 256), axis=0)

    best = jnp.zeros((8, 256), F32)
    for i in range(8):
        copies[i].wait()

        for third in range(3):
            rows = pl.ds(128 * third, 128)
            wide = jnp.concatenate([signs, signs], axis=0)
            mine = buffer[i, core, rows, :] * wide
            own_ref[i, rows, :] = mine
            other = buffer[i, 1 - core, rows, :] * wide
            for v, keep in ((other, True), (mine, False)):
                block = jnp.concatenate([v[:, :256], v[:, 256:]], axis=0)
                turned = jnp.dot(block, table, preferred_element_type=F32)
                if keep:
                    raw_ref[i, rows, :256] = turned[:128] * ROOT
                    raw_ref[i, rows, 256:] = turned[128:] * ROOT
                best = jnp.maximum(best, fold(turned))
    top_ref[...] = jnp.broadcast_to(jnp.max(best, axis=(0, 1), keepdims=True) * ROOT, (128, 128))


VMEM = pl.BlockSpec(memory_space=pltpu.VMEM)


def rotate_half(start, grads, signs, table):
    return pl.pallas_call(
        functools.partial(rotate_kernel, start),
        in_specs=[pl.BlockSpec(memory_space=pl.ANY), VMEM, VMEM],
        out_specs=[VMEM] * 3,
        out_shape=[
            pltpu.VMEM((8, 384, 512), F32),
            pltpu.VMEM((8, 384, 512), BF16),
            jax.ShapeDtypeStruct((128, 128), F32),
        ],
        scratch_shapes=[pltpu.VMEM((8, 2, 384, 512), BF16), pltpu.SemaphoreType.DMA((8,))],
        compiler_params=pltpu.CompilerParams(vmem_limit_bytes=(36 if start else 52) * 2**20),
        cost_estimate=pl.CostEstimate(flops=3 * 10**9, bytes_accessed=13 * 10**6, transcendentals=0),
    )(grads.reshape(16, 2, 384, 512), signs, table)


def nearest(value, unit):
    return jnp.floor(value * (1.0 / unit) + 0.5)


def pack_eight(v):
    last = v[6] + 512.0 * v[7]
    high = nearest(last, 4096.0)
    rest = last - 4096.0 * high
    middle = nearest(rest, 64.0)
    thirds = (high, middle, rest - 64.0 * middle)
    return [(v[2 * i] + 512.0 * v[2 * i + 1]) + 262144.0 * thirds[i] for i in range(3)]


def unpack_eight(words):
    thirds = [nearest(word, 262144.0) for word in words]
    last = (thirds[0] * 4096.0 + thirds[1] * 64.0) + thirds[2]
    values = []
    for pair in [word - 262144.0 * third for word, third in zip(words, thirds)] + [last]:
        upper = nearest(pair, 512.0)
        values += [pair - 512.0 * upper, upper]
    return values


def level_kernel(offset, own0, own1, raw0, raw1, table_ref, top_ref, *outs):
    table = table_ref[...]
    scale = 127.0 / jnp.max(top_ref[...], axis=(0, 1), keepdims=True)
    even = lax.axis_index("core") == 0
    flat = lax.rem(jnp.where(even, lax.axis_index("x"), lax.axis_index("y")) + offset, 4)
    ahead = jnp.where(even, offset, (4 - offset) % 4)
    quarters = [flat, flat, lax.rem(lax.axis_index("z") + ahead, 4)]

    def plane(own_ref, raw_ref, base, step, carry):
        z = base + step
        blocks = [own_ref[4 * step + y, 4 * t + quarters[t]] for t in range(3) for y in range(4)]
        stacked = jnp.concatenate([v[:, 256 * h : 256 * h + 256] for v in blocks for h in range(2)], axis=0)
        mine = jnp.dot(stacked, table, preferred_element_type=F32) * ROOT
        mine = jnp.floor(mine * scale + 0.5)
        for t in range(3):
            for pair in range(2):
                for h in range(2):
                    groups = []
                    for y in (2 * pair, 2 * pair + 1):
                        row = 32 * ((t * 4 + y) * 2 + h)
                        other = raw_ref[4 * step + y, 4 * t + quarters[t], :, 256 * h : 256 * h + 256]
                        total = mine[row : row + 32] + jnp.floor(other * scale + 0.5)
                        groups += [total[8 * g : 8 * g + 8] for g in range(4)]
                    if offset:
                        for i, word in enumerate(pack_eight(groups)):
                            cols = slice(256 * h, 256 * h + 256)
                            if t < 2:
                                outs[0][t, z, pair, i, :, cols] = word
                            else:
                                outs[1][z, pair, i, :, cols] = word
                        continue
                    for k in range(2):
                        low, lower, high, higher = groups[4 * k : 4 * k + 4]
                        word = jnp.concatenate([low + FIELD * high, lower + FIELD * higher], axis=0)
                        for x in range(2):
                            place = outs[0].at[z, 2 * pair + k, 2 * h + x, 16 * t : 16 * t + 16, :]
                            place[...] = word[:, 128 * x : 128 * x + 128]
        return carry

    lax.fori_loop(0, 2, functools.partial(plane, own0, raw0, 0), 0)
    lax.fori_loop(0, 2, functools.partial(plane, own1, raw1, 2), 0)


def levels_for(offset, owns, raws, table, tops):
    shapes = [(2, 4, 2, 3, 8, 512), (4, 2, 3, 8, 512)] if offset else [(4, 4, 4, 48, 128)]
    return pl.pallas_call(
        functools.partial(level_kernel, offset),
        in_specs=[VMEM] * 6,
        out_specs=[VMEM] * len(shapes),
        out_shape=[pltpu.VMEM(shape, F32) for shape in shapes],
        compiler_params=pltpu.CompilerParams(vmem_limit_bytes=12 * 2**20),
        cost_estimate=pl.CostEstimate(flops=10**6, bytes_accessed=10**4, transcendentals=0),
    )(*[part.reshape(8, 12, 32, 512) for part in (*owns, *raws)], table, tops)


def add_plane(z, sums_ref, parts, out_ref):
    for t, part in enumerate(parts):
        for pair in range(2):
            v = unpack_eight([part[z, pair, i] for i in range(3)])
            for k in range(2):
                low, lower, high, higher = v[4 * k : 4 * k + 4]
                for j, word in enumerate((low + FIELD * high, lower + FIELD * higher)):
                    for x in range(4):
                        where = (z, 2 * pair + k, x, pl.ds(16 * t + 8 * j, 8))
                        out_ref[where] = sums_ref[where] + word[:, 128 * x : 128 * x + 128]


def add_kernel(sums_ref, flat_ref, tall_ref, out_ref):
    parts = (flat_ref.at[0], flat_ref.at[1], tall_ref)

    def plane(z, carry):
        add_plane(z, sums_ref, parts, out_ref)
        return carry

    lax.fori_loop(0, 4, plane, 0)


def last_add_kernel(sums_ref, flat_ref, tall_ref, out_ref, buffer, sems):
    parts = (flat_ref.at[0], flat_ref.at[1], tall_ref)
    copies = [pltpu.make_async_copy(buffer.at[z], out_ref.at[z], sems.at[z]) for z in range(4)]
    for z in range(4):
        add_plane(z, sums_ref, parts, buffer)
        copies[z].start()
    for copy in copies:
        copy.wait()


def add_parts(sums, parts, last):
    shape = (4, 4, 4, 48, 128)
    return pl.pallas_call(
        last_add_kernel if last else add_kernel,
        in_specs=[VMEM] * 3,
        out_specs=pl.BlockSpec(memory_space=pl.ANY) if last else VMEM,
        out_shape=jax.ShapeDtypeStruct(shape, F32) if last else pltpu.VMEM(shape, F32),
        scratch_shapes=[pltpu.VMEM(shape, F32), pltpu.SemaphoreType.DMA((4,))] if last else [],
        compiler_params=pltpu.CompilerParams(vmem_limit_bytes=12 * 2**20),
        cost_estimate=pl.CostEstimate(flops=10**7, bytes_accessed=4 * 10**6, transcendentals=0),
    )(sums, *parts)


def update_kernel(
    scalars, words_ref, table_ref, sign_ref, weights_ref, first_ref, second_ref, weights_out, first_out, second_out
):
    table = table_ref[...]
    even = lax.axis_index("core") == 0
    coarse, fine = [], []
    for t in range(3):
        for q in range(4):
            low = high = jnp.zeros((16, 128), F32)
            for a in range(4):
                for b in range(4):
                    z, y, x = (a, jnp.where(even, b, q), jnp.where(even, q, b)) if t < 2 else (q, a, b)
                    word = words_ref[z, y, x, 16 * t : 16 * t + 16, :]
                    upper = nearest(word, FIELD)
                    high = high + upper
                    low = low + (word - upper * FIELD)
            total = jnp.concatenate([low, high], axis=0)
            coarse.append(nearest(total, 128.0))
            fine.append(total - coarse[-1] * 128.0)
    digits = jnp.concatenate(coarse + fine, axis=0).astype(BF16)
    turned = jnp.dot(digits, table, preferred_element_type=F32)
    signs = jnp.concatenate([sign_ref[...].astype(F32)] * 6, axis=0)
    grad = ((128.0 * turned[:384] + turned[384:]) * scalars[0]) * ROOT * signs
    first = 0.9 * first_ref[...] + 0.1 * grad
    second = 0.95 * second_ref[...] + 0.05 * grad * grad
    weights = weights_ref[...]
    update = (first / scalars[1]) / (jnp.sqrt(second / scalars[2]) + 1e-08) + 0.1 * weights
    weights_out[...] = weights - 0.2 * update
    first_out[...] = first
    second_out[...] = second


def shift_flat(amount):
    index = np.arange(128).reshape(4, 4, 4, 2)
    ahead = np.stack([np.roll(index[..., 0], -amount, axis=0), np.roll(index[..., 1], -amount, axis=2)], axis=-1)
    return [(int(source), int(target)) for source, target in zip(index.ravel(), ahead.ravel())]


def shift_tall(amount):
    return [
        (2 * i + core, 2 * ((i + (amount if core == 0 else -amount)) % 4) + core)
        for i in range(4)
        for core in range(2)
    ]


def shards(gradients, sign_table, loss_scale, step_count, weights, first_moment, second_moment):
    grads = gradients[0, 0]
    table = jnp.asarray(hadamard(BLOCK), BF16)
    twice = jnp.asarray(np.kron(np.eye(2, dtype=np.float32), hadamard(BLOCK)), BF16)
    raws, owns, tiles = [], [], []
    for start in (0, 8):
        raw, own, tile = rotate_half(start, grads, sign_table, twice)
        raws.append(lax.ppermute(raw, "core", [(0, 1), (1, 0)]))
        owns.append(own)
        tiles.append(tile)
    tops = lax.all_to_all(jnp.maximum(*tiles), ALL, 0, 0, tiled=True)

    arrived = []
    for offset in (1, 3, 2):
        flat, tall = levels_for(offset, owns, raws, twice, tops)
        flat = lax.ppermute(flat, MESH, shift_flat(offset))
        arrived.append((flat, lax.ppermute(tall, ("z", "core"), shift_tall(offset))))
    (words,) = levels_for(0, owns, raws, twice, tops)
    for number, parts in enumerate(arrived):
        words = add_parts(words, parts, number == 2)
    words = words.reshape(64, 48, 128)
    words = lax.all_to_all(words, CHIPS, 0, 0, tiled=True)

    top_value = jnp.max(tops)
    factor = top_value / (127.0 * 128.0 * loss_scale[0])
    steps_float = step_count[0].astype(F32)
    scalars = jnp.stack(
        [
            factor,
            1.0 - jnp.power(F32(0.9), steps_float),
            1.0 - jnp.power(F32(0.95), steps_float),
        ]
    )
    own_signs = lax.dynamic_slice_in_dim(sign_table, lax.axis_index("x") * BLOCK, BLOCK, 1)
    return pl.pallas_call(
        update_kernel,
        in_specs=[pl.BlockSpec(memory_space=pltpu.SMEM)] + [VMEM] * 6,
        out_specs=[VMEM] * 3,
        out_shape=[jax.ShapeDtypeStruct((384, 128), F32)] * 3,
        compiler_params=pltpu.CompilerParams(vmem_limit_bytes=40 * 2**20),
    )(scalars, words.reshape(4, 4, 4, 48, 128), table, own_signs, weights, first_moment, second_moment)


def solution(mesh):
    torus = Mesh(mesh.devices.reshape(4, 4, 4, 2), ("x", "z", "y", "core"))
    owned = P(INTRA, "x")
    return jax.shard_map(
        shards,
        mesh=torus,
        in_specs=(P("x", INTRA, None, None), P(), P(), P(), owned, owned, owned),
        out_specs=(owned, owned, owned),
        check_vma=False,
    )
```

```python
import functools
import math

import jax
import jax.numpy as jnp
import numpy as np
from jax import lax
from jax.experimental import pallas as pl
from jax.experimental.pallas import tpu as pltpu
from jax.sharding import Mesh
from jax.sharding import PartitionSpec as P

BLOCK = 128
SIGN_ROWS = 64
ROOT = 1.0 / math.sqrt(BLOCK)
CHIPS = ("z", "y", "x")
ALL = ("z", "y", "x", "core")
INTRA = ("z", "y", "core")
MESH = ("x", "z", "y", "core")
FIELD = 4096.0
F32 = jnp.float32
BF16 = jnp.bfloat16


def hadamard(order):
    table = np.ones((1, 1), np.float32)
    while table.shape[0] < order:
        table = np.block([[table, table], [table, -table]])
    return table


def rotate_kernel(start, grads_ref, sign_ref, table_ref, raw_ref, own_ref, top_ref, buffer, sems):
    core = lax.axis_index("core")
    copies = [pltpu.make_async_copy(grads_ref.at[start + i], buffer.at[i], sems.at[i]) for i in range(8)]
    for copy in copies:
        copy.start()
    signs = sign_ref[...].astype(F32).astype(BF16)
    table = table_ref[...]

    def fold(value):
        return jnp.max(jnp.abs(value).reshape(-1, 8, 256), axis=0)

    best = jnp.zeros((8, 256), F32)
    for i in range(8):
        copies[i].wait()

        for third in range(3):
            rows = pl.ds(128 * third, 128)
            wide = jnp.concatenate([signs, signs], axis=0)
            mine = buffer[i, core, rows, :] * wide
            own_ref[i, rows, :] = mine
            other = buffer[i, 1 - core, rows, :] * wide
            for v, keep in ((other, True), (mine, False)):
                block = jnp.concatenate([v[:, :256], v[:, 256:]], axis=0)
                turned = jnp.dot(block, table, preferred_element_type=F32)
                if keep:
                    raw_ref[i, rows, :256] = turned[:128] * ROOT
                    raw_ref[i, rows, 256:] = turned[128:] * ROOT
                best = jnp.maximum(best, fold(turned))
    top_ref[...] = jnp.broadcast_to(jnp.max(best, axis=(0, 1), keepdims=True) * ROOT, (128, 128))


VMEM = pl.BlockSpec(memory_space=pltpu.VMEM)


def rotate_half(start, grads, signs, table):
    return pl.pallas_call(
        functools.partial(rotate_kernel, start),
        in_specs=[pl.BlockSpec(memory_space=pl.ANY), VMEM, VMEM],
        out_specs=[VMEM] * 3,
        out_shape=[
            pltpu.VMEM((8, 384, 512), F32),
            pltpu.VMEM((8, 384, 512), BF16),
            jax.ShapeDtypeStruct((128, 128), F32),
        ],
        scratch_shapes=[pltpu.VMEM((8, 2, 384, 512), BF16), pltpu.SemaphoreType.DMA((8,))],
        compiler_params=pltpu.CompilerParams(vmem_limit_bytes=(36 if start else 52) * 2**20),
        cost_estimate=pl.CostEstimate(flops=3 * 10**9, bytes_accessed=13 * 10**6, transcendentals=0),
    )(grads.reshape(16, 2, 384, 512), signs, table)


def nearest(value, unit):
    return jnp.floor(value * (1.0 / unit) + 0.5)


def pack_eight(v):
    last = v[6] + 512.0 * v[7]
    high = nearest(last, 4096.0)
    rest = last - 4096.0 * high
    middle = nearest(rest, 64.0)
    thirds = (high, middle, rest - 64.0 * middle)
    return [(v[2 * i] + 512.0 * v[2 * i + 1]) + 262144.0 * thirds[i] for i in range(3)]


def unpack_eight(words):
    thirds = [nearest(word, 262144.0) for word in words]
    last = (thirds[0] * 4096.0 + thirds[1] * 64.0) + thirds[2]
    values = []
    for pair in [word - 262144.0 * third for word, third in zip(words, thirds)] + [last]:
        upper = nearest(pair, 512.0)
        values += [pair - 512.0 * upper, upper]
    return values


def level_kernel(offset, own0, own1, raw0, raw1, table_ref, top_ref, *outs):
    table = table_ref[...]
    scale = 127.0 / jnp.max(top_ref[...], axis=(0, 1), keepdims=True)
    even = lax.axis_index("core") == 0
    flat = lax.rem(jnp.where(even, lax.axis_index("x"), lax.axis_index("y")) + offset, 4)
    ahead = jnp.where(even, offset, (4 - offset) % 4)
    quarters = [flat, flat, lax.rem(lax.axis_index("z") + ahead, 4)]

    def plane(own_ref, raw_ref, base, step, carry):
        z = base + step
        blocks = [own_ref[4 * step + y, 4 * t + quarters[t]] for t in range(3) for y in range(4)]
        stacked = jnp.concatenate([v[:, 256 * h : 256 * h + 256] for v in blocks for h in range(2)], axis=0)
        mine = jnp.dot(stacked, table, preferred_element_type=F32) * ROOT
        mine = jnp.floor(mine * scale + 0.5)
        for t in range(3):
            for pair in range(2):
                for h in range(2):
                    groups = []
                    for y in (2 * pair, 2 * pair + 1):
                        row = 32 * ((t * 4 + y) * 2 + h)
                        other = raw_ref[4 * step + y, 4 * t + quarters[t], :, 256 * h : 256 * h + 256]
                        total = mine[row : row + 32] + jnp.floor(other * scale + 0.5)
                        groups += [total[8 * g : 8 * g + 8] for g in range(4)]
                    if offset:
                        for i, word in enumerate(pack_eight(groups)):
                            cols = slice(256 * h, 256 * h + 256)
                            if t < 2:
                                outs[0][t, z, pair, i, :, cols] = word
                            else:
                                outs[1][z, pair, i, :, cols] = word
                        continue
                    for k in range(2):
                        low, lower, high, higher = groups[4 * k : 4 * k + 4]
                        word = jnp.concatenate([low + FIELD * high, lower + FIELD * higher], axis=0)
                        for x in range(2):
                            place = outs[0].at[z, 2 * pair + k, 2 * h + x, 16 * t : 16 * t + 16, :]
                            place[...] = word[:, 128 * x : 128 * x + 128]
        return carry

    lax.fori_loop(0, 2, functools.partial(plane, own0, raw0, 0), 0)
    lax.fori_loop(0, 2, functools.partial(plane, own1, raw1, 2), 0)


def levels_for(offset, owns, raws, table, tops):
    shapes = [(2, 4, 2, 3, 8, 512), (4, 2, 3, 8, 512)] if offset else [(4, 4, 4, 48, 128)]
    return pl.pallas_call(
        functools.partial(level_kernel, offset),
        in_specs=[VMEM] * 6,
        out_specs=[VMEM] * len(shapes),
        out_shape=[pltpu.VMEM(shape, F32) for shape in shapes],
        compiler_params=pltpu.CompilerParams(vmem_limit_bytes=12 * 2**20),
        cost_estimate=pl.CostEstimate(flops=10**6, bytes_accessed=10**4, transcendentals=0),
    )(*[part.reshape(8, 12, 32, 512) for part in (*owns, *raws)], table, tops)


def add_plane(z, sums_ref, parts, out_ref):
    for t, part in enumerate(parts):
        for pair in range(2):
            v = unpack_eight([part[z, pair, i] for i in range(3)])
            for k in range(2):
                low, lower, high, higher = v[4 * k : 4 * k + 4]
                for j, word in enumerate((low + FIELD * high, lower + FIELD * higher)):
                    for x in range(4):
                        where = (z, 2 * pair + k, x, pl.ds(16 * t + 8 * j, 8))
                        out_ref[where] = sums_ref[where] + word[:, 128 * x : 128 * x + 128]


def add_kernel(sums_ref, flat_ref, tall_ref, out_ref):
    parts = (flat_ref.at[0], flat_ref.at[1], tall_ref)

    def plane(z, carry):
        add_plane(z, sums_ref, parts, out_ref)
        return carry

    lax.fori_loop(0, 4, plane, 0)


def last_add_kernel(sums_ref, flat_ref, tall_ref, out_ref, buffer, sems):
    parts = (flat_ref.at[0], flat_ref.at[1], tall_ref)
    copies = [pltpu.make_async_copy(buffer.at[z], out_ref.at[z], sems.at[z]) for z in range(4)]
    for z in range(4):
        add_plane(z, sums_ref, parts, buffer)
        copies[z].start()
    for copy in copies:
        copy.wait()


def add_parts(sums, parts, last):
    shape = (4, 4, 4, 48, 128)
    return pl.pallas_call(
        last_add_kernel if last else add_kernel,
        in_specs=[VMEM] * 3,
        out_specs=pl.BlockSpec(memory_space=pl.ANY) if last else VMEM,
        out_shape=jax.ShapeDtypeStruct(shape, F32) if last else pltpu.VMEM(shape, F32),
        scratch_shapes=[pltpu.VMEM(shape, F32), pltpu.SemaphoreType.DMA((4,))] if last else [],
        compiler_params=pltpu.CompilerParams(vmem_limit_bytes=12 * 2**20),
        cost_estimate=pl.CostEstimate(flops=10**7, bytes_accessed=4 * 10**6, transcendentals=0),
    )(sums, *parts)


def update_kernel(
    scalars, words_ref, table_ref, sign_ref, weights_ref, first_ref, second_ref, weights_out, first_out, second_out
):
    table = table_ref[...]
    even = lax.axis_index("core") == 0
    coarse, fine = [], []
    for t in range(3):
        for q in range(4):
            low = high = jnp.zeros((16, 128), F32)
            for a in range(4):
                for b in range(4):
                    z, y, x = (a, jnp.where(even, b, q), jnp.where(even, q, b)) if t < 2 else (q, a, b)
                    word = words_ref[z, y, x, 16 * t : 16 * t + 16, :]
                    upper = nearest(word, FIELD)
                    high = high + upper
                    low = low + (word - upper * FIELD)
            total = jnp.concatenate([low, high], axis=0)
            coarse.append(nearest(total, 128.0))
            fine.append(total - coarse[-1] * 128.0)
    digits = jnp.concatenate(coarse + fine, axis=0).astype(BF16)
    turned = jnp.dot(digits, table, preferred_element_type=F32)
    signs = jnp.concatenate([sign_ref[...].astype(F32)] * 6, axis=0)
    grad = ((128.0 * turned[:384] + turned[384:]) * scalars[0]) * ROOT * signs
    first = 0.9 * first_ref[...] + 0.1 * grad
    second = 0.95 * second_ref[...] + 0.05 * grad * grad
    weights = weights_ref[...]
    update = (first / scalars[1]) / (jnp.sqrt(second / scalars[2]) + 1e-08) + 0.1 * weights
    weights_out[...] = weights - 0.2 * update
    first_out[...] = first
    second_out[...] = second


def shift_flat(amount):
    index = np.arange(128).reshape(4, 4, 4, 2)
    ahead = np.stack([np.roll(index[..., 0], -amount, axis=0), np.roll(index[..., 1], -amount, axis=2)], axis=-1)
    return [(int(source), int(target)) for source, target in zip(index.ravel(), ahead.ravel())]


def shift_tall(amount):
    return [
        (2 * i + core, 2 * ((i + (amount if core == 0 else -amount)) % 4) + core)
        for i in range(4)
        for core in range(2)
    ]


def shards(gradients, sign_table, loss_scale, step_count, weights, first_moment, second_moment):
    grads = gradients[0, 0]
    table = jnp.asarray(hadamard(BLOCK), BF16)
    twice = jnp.asarray(np.kron(np.eye(2, dtype=np.float32), hadamard(BLOCK)), BF16)
    raws, owns, tiles = [], [], []
    for start in (0, 8):
        raw, own, tile = rotate_half(start, grads, sign_table, twice)
        raws.append(lax.ppermute(raw, "core", [(0, 1), (1, 0)]))
        owns.append(own)
        tiles.append(tile)
    tops = lax.all_to_all(jnp.maximum(*tiles), ALL, 0, 0, tiled=True)

    arrived = []
    for offset in (2, 1, 3):
        flat, tall = levels_for(offset, owns, raws, twice, tops)
        flat = lax.ppermute(flat, MESH, shift_flat(offset))
        arrived.append((flat, lax.ppermute(tall, ("z", "core"), shift_tall(offset))))
    (words,) = levels_for(0, owns, raws, twice, tops)
    for number, parts in enumerate(arrived):
        words = add_parts(words, parts, number == 2)
    words = words.reshape(64, 48, 128)
    words = lax.all_to_all(words, CHIPS, 0, 0, tiled=True)

    top_value = jnp.max(tops)
    factor = top_value / (127.0 * 128.0 * loss_scale[0])
    steps_float = step_count[0].astype(F32)
    scalars = jnp.stack(
        [
            factor,
            1.0 - jnp.power(F32(0.9), steps_float),
            1.0 - jnp.power(F32(0.95), steps_float),
        ]
    )
    own_signs = lax.dynamic_slice_in_dim(sign_table, lax.axis_index("x") * BLOCK, BLOCK, 1)
    return pl.pallas_call(
        update_kernel,
        in_specs=[pl.BlockSpec(memory_space=pltpu.SMEM)] + [VMEM] * 6,
        out_specs=[VMEM] * 3,
        out_shape=[jax.ShapeDtypeStruct((384, 128), F32)] * 3,
        compiler_params=pltpu.CompilerParams(vmem_limit_bytes=40 * 2**20),
    )(scalars, words.reshape(4, 4, 4, 48, 128), table, own_signs, weights, first_moment, second_moment)


def solution(mesh):
    torus = Mesh(mesh.devices.reshape(4, 4, 4, 2), ("x", "z", "y", "core"))
    owned = P(INTRA, "x")
    return jax.shard_map(
        shards,
        mesh=torus,
        in_specs=(P("x", INTRA, None, None), P(), P(), P(), owned, owned, owned),
        out_specs=(owned, owned, owned),
        check_vma=False,
    )
```
